128 devices in a mesh: fsdp: 4 (over z_hi, core), seq: 32 (over y, x, z_lo).
Axes of the slice: x: 4, y: 4, z: 4 (z_hi: 2, z_lo: 2; z = z_hi * 2 + z_lo), core: 2. Of those that a mesh axis runs over, the one named last changes fastest.
Arguments:
- tokens: bfloat16 [4, 8192, 5376], P('fsdp', 'seq'), may hold values from -6 to 6
- norm_gain: float32 [5376], replicated, may hold values from 0.25 to 1.75
- w_query: bfloat16 [5376, 2048], P('fsdp', 'seq'), may hold values from -0.078125 to 0.078125
- w_keyval: bfloat16 [5376, 2048], P('fsdp', 'seq'), may hold values from -0.078125 to 0.078125
- q_gain: float32 [128], replicated, may hold values from 0.5 to 9
- k_gain: float32 [128], replicated, may hold values from 0.5 to 9
Outputs:
- attended: bfloat16 [4, 8192, 2048], P('fsdp', 'seq')
The draws below stay inside these ranges and needn't reach their ends.
All inputs are finite; a program needn't handle non-finite values.
Results may differ from the reference program's by a relative error of at most 0.004.
The reference program's roundings to bfloat16 on the way (of `normed`, `values` and `probs`) count: a program that leaves them out, or rounds other values in their place, can miss the bound.
Values may be sent and summed in bfloat16 or wider, within the bound.
A program may use at most 128 MiB of HBM per device.

```python
import jax
import jax.numpy as jnp
from jax import lax

D = 5376
HQ = 16
HK = 8
HD = 128
WINDOW = 1024
QSCALE = 168
SLABS = 4
SLAB_LEN = 8192
N_FSDP = 4


def draw_q_gain(key, part):
    inner = jax.random.fold_in(key, 11)
    return jax.random.uniform(inner, (HD,), jnp.float32, 0.6, 2.4)


def draw_k_gain(key, part):
    inner = jax.random.fold_in(key, 23)
    return jax.random.uniform(inner, (HD,), jnp.float32, 0.6, 2.4)


def levels(rng, extent, pieces, smallest, largest):
    level = 1.0
    for dim, blocks in pieces:
        draws = jax.random.uniform(jax.random.fold_in(jax.random.fold_in(rng, 6), dim), (blocks,), jnp.float32, smallest / len(pieces), largest / len(pieces))
        level = level * jnp.repeat(jnp.exp(draws), extent[dim] // blocks).reshape((-1,) + (1,) * (len(extent) - 1 - dim))
    return level


def centred(own_key, shape, spread, most, pieces=(), held_as=jnp.bfloat16):
    level = levels(own_key, shape, pieces, -0.22, 0.18) if pieces else 1.0
    entries = jax.random.normal(own_key, shape, jnp.float32) * spread * level
    return jnp.minimum(jnp.maximum(entries, -most), most).astype(held_as)


def setup_inputs(seed: int = 0) -> dict:
    key_list = jax.random.split(jax.random.key(seed), 7)
    tokens = centred(key_list[0], (SLABS, SLAB_LEN, D), 1.0, 6.0, ((0, 4), (1, 32)))
    norm_gain = jnp.clip(1.0 + 0.15 * jax.random.normal(key_list[1], (D,), jnp.float32), 0.25, 1.75)
    w_query = centred(key_list[2], (D, HQ * HD), D ** -0.5, 0.078125, ((0, 4), (1, 32)))
    w_keyval = centred(key_list[3], (D, 2 * HK * HD), D ** -0.5, 0.078125, ((0, 4), (1, 32)))
    q_gain = draw_q_gain(jax.random.fold_in(key_list[6], 71), 0)
    k_gain = draw_k_gain(jax.random.fold_in(key_list[6], 71), 0)
    return dict(tokens=tokens, norm_gain=norm_gain, w_query=w_query, w_keyval=w_keyval, q_gain=q_gain, k_gain=k_gain)


def head_norm(values, gain):
    return values * lax.rsqrt(lax.optimization_barrier(jnp.mean(values * values, axis=-1, keepdims=True)) + 1e-06) * gain

def rotate(values, position):
    half = values.shape[-1] // 2
    index_f = jnp.arange(half).astype(jnp.float32)
    freq = jnp.power(10000.0, -2.0 * index_f / values.shape[-1])
    angle = position[:, None] * freq[None, :]
    cosine = jnp.cos(angle)[:, None, :]
    sine = jnp.sin(angle)[:, None, :]
    first = values[..., :half]
    second = values[..., half:]
    return jnp.concatenate([first * cosine - second * sine, second * cosine + first * sine], axis=-1)

def reference(tokens, norm_gain, w_query, w_keyval, q_gain, k_gain):
    quarter = D // N_FSDP
    groups = HQ // HK
    scale = float(QSCALE) ** (-0.5)
    blocks = SLAB_LEN // WINDOW

    def one_slab(slab):
        flat = slab.astype(jnp.float32)
        normed = (flat * lax.rsqrt(lax.optimization_barrier(jnp.mean(flat * flat, axis=-1, keepdims=True)) + 1e-06) * norm_gain).astype(jnp.bfloat16)
        query_sum = jnp.zeros((SLAB_LEN, HQ * HD), jnp.float32)
        keyval_sum = jnp.zeros((SLAB_LEN, 2 * HK * HD), jnp.float32)
        for part in range(N_FSDP):
            cols = normed[:, part * quarter:(part + 1) * quarter]
            query_sum = query_sum + jnp.dot(cols, w_query[part * quarter:(part + 1) * quarter], preferred_element_type=jnp.float32)
            keyval_sum = keyval_sum + jnp.dot(cols, w_keyval[part * quarter:(part + 1) * quarter], preferred_element_type=jnp.float32)
        position = jnp.arange(SLAB_LEN).astype(jnp.float32)
        query = rotate(head_norm(query_sum.reshape(SLAB_LEN, HQ, HD), q_gain), position)
        keys = rotate(head_norm(keyval_sum[:, :HK * HD].reshape(SLAB_LEN, HK, HD), k_gain), position)
        values = keyval_sum[:, HK * HD:].reshape(SLAB_LEN, HK, HD).astype(jnp.bfloat16)
        keys_pad = jnp.concatenate([jnp.zeros((WINDOW, HK, HD), jnp.float32), keys], axis=0)
        values_pad = jnp.concatenate([jnp.zeros((WINDOW, HK, HD), jnp.bfloat16), values], axis=0)

        def one_block(block):
            start = (block * WINDOW).astype(jnp.int32)
            q_block = lax.dynamic_slice_in_dim(query, start, WINDOW, 0).reshape(WINDOW, HK, groups, HD)
            k_block = lax.dynamic_slice_in_dim(keys_pad, start, 2 * WINDOW, 0)
            v_block = lax.dynamic_slice_in_dim(values_pad, start, 2 * WINDOW, 0)
            scores = jnp.einsum('thgd,khd->hgtk', q_block, k_block, precision=lax.Precision.HIGHEST) * scale
            query_pos = start + jnp.arange(WINDOW).astype(jnp.int32)
            key_pos = start - WINDOW + jnp.arange(2 * WINDOW).astype(jnp.int32)
            gap = query_pos[:, None] - key_pos[None, :]
            allowed = (gap >= 0) & (gap < WINDOW) & (key_pos[None, :] >= 0)
            masked = jnp.where(allowed, scores, -1e+30)
            top = lax.optimization_barrier(jnp.max(masked, axis=-1, keepdims=True))
            weights = jnp.where(allowed, jnp.exp(masked - top), 0.0)
            probs = (weights / lax.optimization_barrier(jnp.sum(weights, axis=-1, keepdims=True))).astype(jnp.bfloat16)
            result = jnp.einsum('hgtk,khd->thgd', probs.astype(jnp.float32), v_block.astype(jnp.float32))
            return result.astype(jnp.bfloat16).reshape(WINDOW, HQ * HD)
        outputs = lax.map(one_block, jnp.arange(blocks).astype(jnp.int32))
        return outputs.reshape(SLAB_LEN, HQ * HD)
    return lax.map(one_slab, tokens)
```

```python
import functools
import math

import jax
import jax.numpy as jnp
from jax import lax
from jax.experimental import pallas as pl
from jax.experimental.pallas import tpu as pltpu
from jax.sharding import PartitionSpec as P

WINDOW = 1024
QSCALE = 168
MESH = pl.DeviceIdType.MESH
F32 = jnp.float32
BF16 = jnp.bfloat16
NEG = -1e30

ORDERS = (("x", "y", "z"), ("y", "z", "x"), ("z", "x", "y"))


def position():
    f, s = lax.axis_index("fsdp"), lax.axis_index("seq")
    return {"x": (s // 2) % 4, "y": s // 8, "z": 2 * (f // 2) + s % 2}, f % 2


def device(at, core):
    return (2 * (at["z"] // 2) + core, 8 * at["y"] + 2 * at["x"] + at["z"] % 2)


def shifted(at, dim, by):
    moved = dict(at)
    moved[dim] = (at[dim] + by + 4) % 4
    return moved


def project_kernel(
    tok_ref, gain_ref, shard_ref, cos_ref, sin_ref, ga_ref, gb_ref,
    q_ref, kv_ref,
    w0, w1, w2, normed, spread, acc, other, local_sem, ring_send, ring_recv,
    tok_send, tok_recv, part_send, part_recv,
):
    at, core = position()
    me = device(at, core)
    partner = device(at, 1 - core)
    rows = tok_ref.shape[0]
    third = w0.shape[3]
    weights = (w0, w1, w2)

    barrier = pltpu.get_barrier_semaphore()
    peers = [device(shifted(at, d, by), core) for d in "xyz" for by in (1, -1)] + [partner]
    for peer in peers:
        pl.semaphore_signal(barrier, inc=1, device_id=peer, device_id_type=MESH)

    own = []
    for c, (d1, d2, d3) in enumerate(ORDERS):
        own.append(pltpu.make_async_copy(
            shard_ref.at[c], weights[c].at[at[d3], at[d2], at[d1]], local_sem.at[c]))
        own[-1].start()
    for copy in own:
        copy.wait()
    pl.semaphore_wait(barrier, len(peers))

    sent = []

    def view(c, phase, index, half):
        d1, d2, d3 = ORDERS[c]
        w = weights[c]
        if phase == 0:
            if half is None:
                return w.at[at[d3], at[d2], index]
            return w.at[at[d3], at[d2], index, pl.ds(half * (third // 2), third // 2)]
        if phase == 1:
            if half is None:
                return w.at[at[d3], index]
            return w.at[at[d3], index, pl.ds(2 * half, 2)]
        if half is None:
            return w.at[index]
        return w.at[index, pl.ds(2 * half, 2)]

    def ring(c, phase, step):
        dim = ORDERS[c][phase]
        copies = []
        for side, by in enumerate((1, -1)):
            if step == 0:
                block = view(c, phase, at[dim], None)
            else:
                block = view(c, phase, shifted(at, dim, -by)[dim], side)
            copies.append(pltpu.make_async_remote_copy(
                src_ref=block, dst_ref=block,
                send_sem=ring_send.at[c, phase, step, side],
                recv_sem=ring_recv.at[c, phase, step, side],
                device_id=device(shifted(at, dim, by), core), device_id_type=MESH))
        return copies

    def start(copies):
        for copy in copies:
            copy.start()
        sent.extend(copies)

    flying = [ring(c, 0, 0) for c in range(3)]
    for copies in flying:
        start(copies)
    for phase in range(3):
        for step in range(2):
            if (phase, step) == (2, 0):
                break
            later = (phase, 1) if step == 0 else (phase + 1, 0)
            for c in range(3):
                for copy in flying[c]:
                    copy.wait_recv()
                flying[c] = ring(c, *later)
                start(flying[c])

    strip = 32

    def norm_rows(i, _):
        at_row = pl.ds(pl.multiple_of(i * strip, strip), strip)
        flat = tok_ref[at_row, :].astype(F32)
        mean = jnp.mean(flat * flat, axis=-1, keepdims=True)
        out = (flat * lax.rsqrt(mean + 1e-6) * gain_ref[...]).astype(BF16)
        for q in range(4):
            for c in range(3):
                k = q * 3 + c
                normed[q, c, at_row, :] = out[:, k * third:(k + 1) * third]
        return 0

    lax.fori_loop(0, rows // strip, norm_rows, 0)
    exchange = []
    for zh in range(2):
        pltpu_copy = pltpu.make_async_copy(
            normed.at[2 * zh + core], spread.at[zh, core], local_sem.at[3 + zh])
        pltpu_copy.start()
        remote = pltpu.make_async_remote_copy(
            src_ref=normed.at[2 * zh + 1 - core], dst_ref=spread.at[zh, core],
            send_sem=tok_send.at[zh], recv_sem=tok_recv.at[zh],
            device_id=partner, device_id_type=MESH)
        remote.start()
        exchange.append((pltpu_copy, remote))
    for mine, remote in exchange:
        mine.wait()
        remote.wait()

    x, y, zown = at["x"], at["y"], at["z"] // 2

    def weight(c, z, yy, xx):
        index = {"x": xx, "y": yy, "z": z}
        d1, d2, d3 = ORDERS[c]
        return weights[c][index[d3], index[d2], index[d1]]

    def units(yy, xx, parts, first):
        h = 4 * yy + xx
        for slab in range(2):
            total = None
            for c, zh in parts:
                rhs = jnp.concatenate(
                    [weight(c, 2 * zh, yy, xx), weight(c, 2 * zh + 1, yy, xx)], axis=1)
                term = jnp.dot(spread[zh, slab, c], rhs, preferred_element_type=F32)
                total = term if total is None else total + term
            if first:
                acc[h, slab] = total
            else:
                acc[h, slab] += total

    def near(k):
        return k + k // 2

    zfar = 1 - zown
    both = lambda c: [(c, 0), (c, 1)]

    def wait_ring():
        for c in range(3):
            for copy in flying[c]:
                copy.wait_recv()

    wait_ring()
    for c in range(3):
        flying[c] = ring(c, 2, 1)
        start(flying[c])

    def early_near(i, _):
        units((y + near(i // 3)) % 4, (x + near(i % 3)) % 4, [(0, zown)] + both(1) + both(2), True)
        return 0

    def early_x(i, _):
        units((y + near(i)) % 4, (x + 2) % 4, [(0, zown)] + both(2), True)
        return 0

    def early_y(i, _):
        units((y + 2) % 4, (x + near(i)) % 4, [(0, zown)] + both(1), True)
        return 0

    lax.fori_loop(0, 9, early_near, 0)
    lax.fori_loop(0, 3, early_x, 0)
    lax.fori_loop(0, 3, early_y, 0)
    units((y + 2) % 4, (x + 2) % 4, [(0, zown)], True)
    wait_ring()

    def part(h):
        return pltpu.make_async_remote_copy(
            src_ref=acc.at[h, 1 - core], dst_ref=other.at[h],
            send_sem=part_send.at[h], recv_sem=part_recv.at[h],
            device_id=partner, device_id_type=MESH)

    def late(h):
        part(h).start()

    def late_near(i, _):
        yy, xx = (y + near(i // 3)) % 4, (x + near(i % 3)) % 4
        units(yy, xx, [(0, zfar)], False)
        late(4 * yy + xx)
        return 0

    def late_x(i, _):
        yy, xx = (y + near(i)) % 4, (x + 2) % 4
        units(yy, xx, [(0, zfar)] + both(1), False)
        late(4 * yy + xx)
        return 0

    def late_y(i, _):
        yy, xx = (y + 2) % 4, (x + near(i)) % 4
        units(yy, xx, [(0, zfar)] + both(2), False)
        late(4 * yy + xx)
        return 0

    lax.fori_loop(0, 9, late_near, 0)
    lax.fori_loop(0, 3, late_x, 0)
    lax.fori_loop(0, 3, late_y, 0)
    units((y + 2) % 4, (x + 2) % 4, [(0, zfar)] + both(1) + both(2), False)
    late(4 * ((y + 2) % 4) + (x + 2) % 4)

    half = 64
    low = lax.broadcasted_iota(jnp.int32, (rows, 2 * half), 1) < half

    def head(h, is_key):
        part(h).wait_recv()
        p0 = acc[h, core, :, 0:128] + other[h, :, 0:128]
        p1 = acc[h, core, :, 128:256] + other[h, :, 128:256]
        squares = p0 * p0 + p1 * p1
        mean_q = jnp.sum(jnp.where(low, squares, 0.0), axis=-1, keepdims=True) / 128.0
        rq = lax.rsqrt(mean_q + 1e-6)
        if is_key:
            mean_k = jnp.sum(jnp.where(low, 0.0, squares), axis=-1, keepdims=True) / 128.0
            r = jnp.where(low, rq, lax.rsqrt(mean_k + 1e-6))
        else:
            r = rq
        n0 = p0 * r * ga_ref[...]
        n1 = p1 * r * gb_ref[...]
        cos, sin = cos_ref[...], sin_ref[...]
        r0 = n0 * cos - n1 * sin
        r1 = n1 * cos + n0 * sin
        q = jnp.where(low, r0, pltpu.roll(r1, half, 1)) * (QSCALE ** -0.5 * math.log2(math.e))
        q_hi = q.astype(BF16)
        q_ref[h, :, 0:128] = q_hi
        q_ref[h, :, 128:256] = (q - q_hi.astype(F32)).astype(BF16)
        if is_key:
            k = jnp.where(low, pltpu.roll(r0, half, 1), r1)
            k_hi = k.astype(BF16)
            kv_ref[h, :, 0:128] = k_hi
            kv_ref[h, :, 128:256] = (k - k_hi.astype(F32)).astype(BF16)
        else:
            v = jnp.where(low, pltpu.roll(p0, half, 1), p1)
            kv_ref[h - 8, :, 256:384] = v.astype(BF16)

    def key_head(h, _):
        head(h, True)
        return 0

    def value_head(h, _):
        head(h, False)
        return 0

    lax.fori_loop(0, 8, key_head, 0)
    lax.fori_loop(8, 16, value_head, 0)
    for copy in sent:
        copy.wait_send()

    def drain(h, _):
        part(h).wait_send()
        return 0

    lax.fori_loop(0, 16, drain, 0)


def attend_kernel(q_ref, own_ref, out_ref, kv, own_sem, send_sem, recv_sem):
    f, s = lax.axis_index("fsdp"), lax.axis_index("seq")
    zlo = s % 2
    count = lax.axis_size("seq")
    rows = own_ref.shape[1]
    groups = 4
    per = own_ref.shape[0] // groups
    ahead, pair = s + 2, s + 1 - 2 * zlo

    barrier = pltpu.get_barrier_semaphore()

    def greet(target):
        pl.semaphore_signal(barrier, inc=1, device_id=(f, target), device_id_type=MESH)

    for target in (pair, (s + 2) % count, (s - 2 + count) % count):
        greet(target)

    own = pltpu.make_async_copy(own_ref, kv.at[0], own_sem)
    own.start()

    def clear(slot, absent):
        @pl.when(absent)
        def _():
            kv[slot] = jnp.zeros(kv.shape[1:], BF16)

    clear(1, s < 1)
    clear(2, s < 2)
    clear(3, s < 3)
    clear(4, s < 4)
    own.wait()
    pl.semaphore_wait(barrier, 3)

    def move(src, dst, group, target):
        block = pl.ds(group * per, per)
        return pltpu.make_async_remote_copy(
            src_ref=kv.at[src, block], dst_ref=kv.at[dst, block],
            send_sem=send_sem.at[dst, group], recv_sem=recv_sem.at[dst, group],
            device_id=(f, target), device_id_type=MESH)

    def arrived(slot, group):
        move(slot, slot, group, pair).wait_recv()

    sends = (
        (ahead < count, 0, 2, ahead),
        ((s >= 2) & (ahead < count), 2, 4, ahead),
        (zlo == 0, 0, 1, pair),
        ((zlo == 0) & (s >= 2), 2, 3, pair),
        ((zlo == 1) & (s >= 2), 2, 1, pair),
        ((zlo == 1) & (s >= 4), 4, 3, pair),
    )

    def send(which, group):
        condition, src, dst, target = sends[which]

        @pl.when(condition)
        def _():
            move(src, dst, group, target).start()

    def drain(which, group):
        condition, src, dst, target = sends[which]

        @pl.when(condition)
        def _():
            move(src, dst, group, target).wait_send()

    def receive(slot, group):
        @pl.when(s >= slot)
        def _():
            arrived(slot, group)

    row = lax.broadcasted_iota(jnp.int32, (rows, rows), 0)
    col = lax.broadcasted_iota(jnp.int32, (rows, rows), 1)
    causal = col <= row
    contract = (((1,), (1,)), ((), ()))
    pen = [jnp.where(s >= slot, 0.0, NEG).astype(F32) for slot in range(5)]

    def query_head(h, k):
        q_hi, q_lo = q_ref[h, :, 0:128], q_ref[h, :, 128:256]
        q_hi, q_lo = jnp.concatenate([q_hi, q_hi], 1), jnp.concatenate([q_lo, q_lo], 1)

        def score(slot):
            keys = kv[slot, k, :, 0:256]
            return (lax.dot_general(q_hi, keys, contract, preferred_element_type=F32)
                    + lax.dot_general(q_lo, keys, contract, preferred_element_type=F32))

        edge = jnp.where(causal, score(0), score(4) + pen[4])
        inner = [score(slot) for slot in (1, 2, 3)]
        top = jnp.max(edge, axis=-1, keepdims=True)
        for slot in (1, 2, 3):
            top = jnp.maximum(top, jnp.max(inner[slot - 1], axis=-1, keepdims=True) + pen[slot])
        w_edge = jnp.exp2(edge - top)
        w_inner = [jnp.exp2(inner[slot - 1] - (top - pen[slot])) for slot in (1, 2, 3)]
        total = jnp.sum(w_edge, axis=-1, keepdims=True)
        for w in w_inner:
            total = total + jnp.sum(w, axis=-1, keepdims=True)
        inv = 1.0 / total
        p_edge = w_edge * inv
        out = jnp.dot(jnp.where(causal, p_edge, 0.0).astype(BF16), kv[0, k, :, 256:384],
                      preferred_element_type=F32)
        out += jnp.dot(jnp.where(causal, 0.0, p_edge).astype(BF16), kv[4, k, :, 256:384],
                       preferred_element_type=F32)
        for slot in (1, 2, 3):
            out += jnp.dot((w_inner[slot - 1] * inv).astype(BF16), kv[slot, k, :, 256:384],
                           preferred_element_type=F32)
        out_ref[:, pl.ds(pl.multiple_of(h * 128, 128), 128)] = out.astype(BF16)

    def attend(group):
        def body(i, _):
            h = group * per * 2 + i
            query_head(h, h // 2)
            return 0

        lax.fori_loop(0, 2 * per, body, 0)

    for g in (0, 1):
        send(0, g)
        send(2, g)
    for g in range(groups):
        receive(2, g)
        send(1, g)
        send(3, g)
        send(4, g)
        if g + 2 < groups:
            send(0, g + 2)
            send(2, g + 2)
        receive(4, g)
        send(5, g)
        if g >= 1:
            receive(1, g - 1)
            receive(3, g - 1)
            attend(g - 1)
    receive(1, groups - 1)
    receive(3, groups - 1)
    attend(groups - 1)
    for which in range(len(sends)):
        for g in range(groups):
            drain(which, g)


def on_device(tokens, norm_gain, w_query, w_keyval, q_gain, k_gain):
    rows, width = tokens.shape[1:]
    quarter, cols = w_query.shape
    heads = cols * lax.axis_size("seq") // q_gain.shape[0]
    half = q_gain.shape[0] // 2
    third = quarter // 3
    shard = jnp.concatenate([w_query, w_keyval], axis=1).reshape(3, third, 2 * cols)
    place = (lax.axis_index("seq") * rows + jnp.arange(rows)).astype(F32)
    freq = jnp.power(10000.0, -2.0 * jnp.arange(half).astype(F32) / (2 * half))
    angle = place[:, None] * freq[None, :]
    cos = jnp.tile(jnp.cos(angle), (1, 2))
    sin = jnp.tile(jnp.sin(angle), (1, 2))
    ga = jnp.concatenate([q_gain[:half], k_gain[:half]])[None]
    gb = jnp.concatenate([q_gain[half:], k_gain[half:]])[None]
    vmem = pl.BlockSpec(memory_space=pltpu.VMEM)
    anyspace = pl.BlockSpec(memory_space=pl.ANY)
    dma = pltpu.SemaphoreType.DMA
    block = pltpu.VMEM((4, 4, 4, third, 128), BF16)
    q, kv = pl.pallas_call(
        project_kernel,
        name="project",
        out_shape=(
            jax.ShapeDtypeStruct((heads, rows, 256), BF16),
            jax.ShapeDtypeStruct((heads // 2, rows, 384), BF16),
        ),
        in_specs=[vmem, vmem, anyspace, vmem, vmem, vmem, vmem],
        out_specs=(vmem, vmem),
        scratch_shapes=[
            block, block, block,
            pltpu.VMEM((4, 3, rows, third), BF16),
            pltpu.VMEM((2, 2, 3, rows, third), BF16),
            pltpu.VMEM((heads, 2, rows, 256), F32),
            pltpu.VMEM((heads, rows, 256), F32),
            dma((5,)), dma((3, 3, 2, 2)), dma((3, 3, 2, 2)),
            dma((2,)), dma((2,)), dma((heads,)), dma((heads,)),
        ],
        compiler_params=pltpu.CompilerParams(
            collective_id=0, has_side_effects=True, vmem_limit_bytes=63 * 2**20),
    )(tokens[0], norm_gain[None], shard, cos, sin, ga, gb)
    out = pl.pallas_call(
        attend_kernel,
        name="attend",
        out_shape=jax.ShapeDtypeStruct((rows, heads * 128), BF16),
        in_specs=[vmem, anyspace],
        out_specs=vmem,
        scratch_shapes=[
            pltpu.VMEM((5, heads // 2, rows, 384), BF16),
            dma, dma((5, 4)), dma((5, 4)),
        ],
        compiler_params=pltpu.CompilerParams(
            collective_id=1, has_side_effects=True, vmem_limit_bytes=48 * 2**20),
    )(q, kv)
    return out[None]


def solution(mesh):
    in_specs = (P("fsdp", "seq", None), P(), P("fsdp", "seq"), P("fsdp", "seq"), P(), P())
    out_specs = P("fsdp", "seq", None)
    return jax.shard_map(
        on_device, mesh=mesh, in_specs=in_specs, out_specs=out_specs, check_vma=False
    )
```

```python
import functools
import math

import jax
import jax.numpy as jnp
from jax import lax
from jax.experimental import pallas as pl
from jax.experimental.pallas import tpu as pltpu
from jax.sharding import PartitionSpec as P

WINDOW = 1024
QSCALE = 168
MESH = pl.DeviceIdType.MESH
F32 = jnp.float32
BF16 = jnp.bfloat16
NEG = -1e30

ORDERS = (("x", "y", "z"), ("y", "z", "x"), ("z", "x", "y"))


def position():
    f, s = lax.axis_index("fsdp"), lax.axis_index("seq")
    return {"x": (s // 2) % 4, "y": s // 8, "z": 2 * (f // 2) + s % 2}, f % 2


def device(at, core):
    return (2 * (at["z"] // 2) + core, 8 * at["y"] + 2 * at["x"] + at["z"] % 2)


def shifted(at, dim, by):
    moved = dict(at)
    moved[dim] = (at[dim] + by + 4) % 4
    return moved


def layer_kernel(
    tok_ref, gain_ref, shard_ref, cos_ref, sin_ref, ga_ref, gb_ref,
    out_ref,
    w0, w1, w2, normed, spread, acc, other, q_own, q_in, kv_out, kv, relay, result,
    local_sem, ring_send, ring_recv, tok_send, tok_recv, part_send, part_recv,
    pair_send, pair_recv, x_send, x_recv, relay_recv, out_send, out_recv,
):
    at, core = position()
    me = device(at, core)
    partner = device(at, 1 - core)
    rows = tok_ref.shape[0]
    third = w0.shape[3]
    weights = (w0, w1, w2)
    f, s = lax.axis_index("fsdp"), lax.axis_index("seq")
    zlo = s % 2
    run = s // 2
    runs = 16

    relayed = 4 * at["y"] + (at["x"] + 1) % 4
    relay_to = (f, 2 * ((relayed + 2) % runs) + zlo)
    relay_by = device(shifted(at, "x", -1), core)
    ahead = (f, (s + 2) % (2 * runs))
    behind = (f, (s - 2 + 2 * runs) % (2 * runs))
    pair = (f, s + 1 - 2 * zlo)
    source = (run - 2 + runs) % runs
    relay_from = (f, 2 * (4 * (source // 4) + (source + 3) % 4) + zlo)

    barrier = pltpu.get_barrier_semaphore()
    peers = [device(shifted(at, d, by), core) for d in "xyz" for by in (1, -1)]
    peers += [partner, ahead, behind, relay_to, relay_from]
    for peer in peers:
        pl.semaphore_signal(barrier, inc=1, device_id=peer, device_id_type=MESH)

    def clear(first, absent):
        @pl.when(absent)
        def _():
            kv[:, first:first + 2] = jnp.zeros((4, 2) + kv.shape[2:], BF16)

    clear(0, run < 2)
    clear(2, run < 1)

    own = []
    for c, (d1, d2, d3) in enumerate(ORDERS):
        own.append(pltpu.make_async_copy(
            shard_ref.at[c], weights[c].at[at[d3], at[d2], at[d1]], local_sem.at[c]))
        own[-1].start()
    for copy in own:
        copy.wait()
    pl.semaphore_wait(barrier, len(peers))

    sent = []

    def view(c, phase, index, half):
        d1, d2, d3 = ORDERS[c]
        w = weights[c]
        if phase == 0:
            if half is None:
                return w.at[at[d3], at[d2], index]
            return w.at[at[d3], at[d2], index, pl.ds(half * (third // 2), third // 2)]
        if phase == 1:
            if half is None:
                return w.at[at[d3], index]
            return w.at[at[d3], index, pl.ds(2 * half, 2)]
        if half is None:
            return w.at[index]
        return w.at[index, pl.ds(2 * half, 2)]

    def ring(c, phase, step):
        dim = ORDERS[c][phase]
        copies = []
        for side, by in enumerate((1, -1)):
            if step == 0:
                block = view(c, phase, at[dim], None)
            else:
                block = view(c, phase, shifted(at, dim, -by)[dim], side)
            copies.append(pltpu.make_async_remote_copy(
                src_ref=block, dst_ref=block,
                send_sem=ring_send.at[c, phase, step, side],
                recv_sem=ring_recv.at[c, phase, step, side],
                device_id=device(shifted(at, dim, by), core), device_id_type=MESH))
        return copies

    def start(copies):
        for copy in copies:
            copy.start()
        sent.extend(copies)

    flying = [ring(c, 0, 0) for c in range(3)]
    for copies in flying:
        start(copies)
    for phase in range(3):
        for step in range(2):
            if (phase, step) == (2, 0):
                break
            later = (phase, 1) if step == 0 else (phase + 1, 0)
            for c in range(3):
                for copy in flying[c]:
                    copy.wait_recv()
                flying[c] = ring(c, *later)
                start(flying[c])

    strip = 32

    def norm_rows(i, _):
        at_row = pl.ds(pl.multiple_of(i * strip, strip), strip)
        flat = tok_ref[at_row, :].astype(F32)
        mean = jnp.mean(flat * flat, axis=-1, keepdims=True)
        out = (flat * lax.rsqrt(mean + 1e-6) * gain_ref[...]).astype(BF16)
        for q in range(4):
            for c in range(3):
                k = q * 3 + c
                normed[q, c, at_row, :] = out[:, k * third:(k + 1) * third]
        return 0

    lax.fori_loop(0, rows // strip, norm_rows, 0)
    exchange = []
    for zh in range(2):
        pltpu_copy = pltpu.make_async_copy(
            normed.at[2 * zh + core], spread.at[zh, core], local_sem.at[3 + zh])
        pltpu_copy.start()
        remote = pltpu.make_async_remote_copy(
            src_ref=normed.at[2 * zh + 1 - core], dst_ref=spread.at[zh, core],
            send_sem=tok_send.at[zh], recv_sem=tok_recv.at[zh],
            device_id=partner, device_id_type=MESH)
        remote.start()
        exchange.append((pltpu_copy, remote))
    for mine, remote in exchange:
        mine.wait()
        remote.wait()

    x, y, zown = at["x"], at["y"], at["z"] // 2

    def weight(c, z, yy, xx):
        index = {"x": xx, "y": yy, "z": z}
        d1, d2, d3 = ORDERS[c]
        return weights[c][index[d3], index[d2], index[d1]]

    def units(yy, xx, parts, first):
        h = 4 * yy + xx
        for slab in range(2):
            total = None
            for c, zh in parts:
                rhs = jnp.concatenate(
                    [weight(c, 2 * zh, yy, xx), weight(c, 2 * zh + 1, yy, xx)], axis=1)
                term = jnp.dot(spread[zh, slab, c], rhs, preferred_element_type=F32)
                total = term if total is None else total + term
            if first:
                acc[h, slab] = total
            else:
                acc[h, slab] += total

    def near(k):
        return k + k // 2

    zfar = 1 - zown
    both = lambda c: [(c, 0), (c, 1)]

    def wait_ring():
        for c in range(3):
            for copy in flying[c]:
                copy.wait_recv()

    wait_ring()
    for c in range(3):
        flying[c] = ring(c, 2, 1)
        start(flying[c])

    def early_near(i, _):
        units((y + near(i // 3)) % 4, (x + near(i % 3)) % 4, [(0, zown)] + both(1) + both(2), True)
        return 0

    def early_x(i, _):
        units((y + near(i)) % 4, (x + 2) % 4, [(0, zown)] + both(2), True)
        return 0

    def early_y(i, _):
        units((y + 2) % 4, (x + near(i)) % 4, [(0, zown)] + both(1), True)
        return 0

    lax.fori_loop(0, 9, early_near, 0)
    lax.fori_loop(0, 3, early_x, 0)
    lax.fori_loop(0, 3, early_y, 0)
    units((y + 2) % 4, (x + 2) % 4, [(0, zown)], True)
    wait_ring()

    def part(h):
        return pltpu.make_async_remote_copy(
            src_ref=acc.at[h, 1 - core], dst_ref=other.at[h],
            send_sem=part_send.at[h], recv_sem=part_recv.at[h],
            device_id=partner, device_id_type=MESH)

    def late(h):
        part(h).start()

    def late_near(i, _):
        yy, xx = (y + near(i // 3)) % 4, (x + near(i % 3)) % 4
        units(yy, xx, [(0, zfar)], False)
        late(4 * yy + xx)
        return 0

    def late_x(i, _):
        yy, xx = (y + near(i)) % 4, (x + 2) % 4
        units(yy, xx, [(0, zfar)] + both(1), False)
        late(4 * yy + xx)
        return 0

    def late_y(i, _):
        yy, xx = (y + 2) % 4, (x + near(i)) % 4
        units(yy, xx, [(0, zfar)] + both(2), False)
        late(4 * yy + xx)
        return 0

    lax.fori_loop(0, 9, late_near, 0)
    lax.fori_loop(0, 3, late_x, 0)
    lax.fori_loop(0, 3, late_y, 0)
    units((y + 2) % 4, (x + 2) % 4, [(0, zfar)] + both(1) + both(2), False)
    late(4 * ((y + 2) % 4) + (x + 2) % 4)

    half = 64
    low = lax.broadcasted_iota(jnp.int32, (rows, 2 * half), 1) < half

    def head(h, keep_kv, is_key):
        part(h).wait_recv()
        p0 = acc[h, core, :, 0:128] + other[h, :, 0:128]
        p1 = acc[h, core, :, 128:256] + other[h, :, 128:256]
        squares = p0 * p0 + p1 * p1
        mean_q = jnp.sum(jnp.where(low, squares, 0.0), axis=-1, keepdims=True) / 128.0
        rq = lax.rsqrt(mean_q + 1e-6)
        if is_key:
            mean_k = jnp.sum(jnp.where(low, 0.0, squares), axis=-1, keepdims=True) / 128.0
            r = jnp.where(low, rq, lax.rsqrt(mean_k + 1e-6))
        else:
            r = rq
        n0 = p0 * r * ga_ref[...]
        n1 = p1 * r * gb_ref[...]
        cos, sin = cos_ref[...], sin_ref[...]
        r0 = n0 * cos - n1 * sin
        r1 = n1 * cos + n0 * sin
        q = jnp.where(low, r0, pltpu.roll(r1, half, 1)) * (QSCALE ** -0.5 * math.log2(math.e))
        q_hi = q.astype(BF16)
        q_own[h, :, 0:128] = q_hi
        q_own[h, :, 128:256] = (q - q_hi.astype(F32)).astype(BF16)
        if is_key:
            k = jnp.where(low, pltpu.roll(r0, half, 1), r1)
            k_hi = k.astype(BF16)
            keep_kv[:, 0:128] = k_hi
            keep_kv[:, 128:256] = (k - k_hi.astype(F32)).astype(BF16)
        else:
            v = jnp.where(low, pltpu.roll(p0, half, 1), p1)
            keep_kv[:, 256:384] = v.astype(BF16)

    def remote(src, dst, send_sem, recv_sem, to):
        return pltpu.make_async_remote_copy(
            src_ref=src, dst_ref=dst, send_sem=send_sem, recv_sem=recv_sem,
            device_id=to, device_id_type=MESH)

    def over_pair(g):
        return remote(kv_out.at[g], kv.at[g, 4 + zlo], pair_send.at[0, g], pair_recv.at[0, g], pair)

    def query_pair(g):
        mine = pl.ds(8 * (1 - zlo) + 2 * g, 2)
        return remote(q_own.at[mine], q_in.at[pl.ds(2 * g, 2)],
                      pair_send.at[1, g], pair_recv.at[1, g], pair)

    def next_run(g, block):
        return remote(kv.at[g, 4 + block], kv.at[g, 2 + block],
                      x_send.at[block, g], x_recv.at[2 + block, g], ahead)

    def second_run(g):
        return remote(kv.at[g, 2], kv.at[g, 0], x_send.at[2, g], x_recv.at[0, g], ahead)

    def to_relay(g):
        return remote(kv.at[g, 5], relay.at[g], x_send.at[3, g], relay_recv.at[g], relay_by)

    def from_relay(g):
        return remote(relay.at[g], kv.at[g, 1], x_send.at[4, g], x_recv.at[1, g], relay_to)

    def when(condition, action):
        @pl.when(condition)
        def _():
            action()

    has_next, has_second = run + 1 < runs, run + 2 < runs
    relays = relayed + 2 < runs

    def send_own(g):
        when(has_next, next_run(g, zlo).start)
        when(has_second & (zlo == 1), to_relay(g).start)

    def hop(g):
        over_pair(g).wait_recv()
        when(has_next, next_run(g, 1 - zlo).start)
        when(has_second & (zlo == 0), to_relay(g).start)

    def forward(g):
        when(run >= 1, next_run(g, 0).wait_recv)
        when((run >= 1) & has_next, second_run(g).start)
        when(relays, to_relay(g).wait_recv)
        when(relays, from_relay(g).start)

    def epilogue(g, _):
        for mine in (True, False):
            k = 4 * zlo + g if mine else 4 * (1 - zlo) + g
            keep = kv.at[g, 4 + zlo] if mine else kv_out.at[g]
            head(k, keep, True)
            head(8 + k, keep, False)
        over_pair(g).start()
        when(g < 2, lambda: send_own(g))
        return 0

    lax.fori_loop(0, 4, epilogue, 0)
    for g in range(4):
        query_pair(g).start()

    row = lax.broadcasted_iota(jnp.int32, (rows, rows), 0)
    col = lax.broadcasted_iota(jnp.int32, (rows, rows), 1)
    causal = col <= row
    contract = (((1,), (1,)), ((), ()))

    def query_head(g, token_block, q, keep):
        q_hi, q_lo = q[:, 0:128], q[:, 128:256]
        q_hi, q_lo = jnp.concatenate([q_hi, q_hi], 1), jnp.concatenate([q_lo, q_lo], 1)
        pen = [jnp.where(2 * run - 4 + token_block + m >= 0, 0.0, NEG).astype(F32)
               for m in range(5)]

        def score(m):
            keys = kv[g, token_block + m, :, 0:256]
            return (lax.dot_general(q_hi, keys, contract, preferred_element_type=F32)
                    + lax.dot_general(q_lo, keys, contract, preferred_element_type=F32))

        def attend_to(probs, m):
            return jnp.dot(probs.astype(BF16), kv[g, token_block + m, :, 256:384],
                           preferred_element_type=F32)

        edge = jnp.where(causal, score(4), score(0) + pen[0])
        inner = {m: score(m) for m in (1, 2, 3)}
        top = jnp.max(edge, axis=-1, keepdims=True)
        for m in inner:
            top = jnp.maximum(top, jnp.max(inner[m], axis=-1, keepdims=True) + pen[m])
        w_edge = jnp.exp2(edge - top)
        w_inner = {m: jnp.exp2(inner[m] - (top - pen[m])) for m in inner}
        total = jnp.sum(w_edge, axis=-1, keepdims=True)
        for m in inner:
            total = total + jnp.sum(w_inner[m], axis=-1, keepdims=True)
        inv = 1.0 / total
        p_edge = w_edge * inv
        out = attend_to(jnp.where(causal, p_edge, 0.0), 4)
        out += attend_to(jnp.where(causal, 0.0, p_edge), 0)
        for m in inner:
            out += attend_to(w_inner[m] * inv, m)
        keep[...] = out.astype(BF16)

    def columns(g):
        return out_ref.at[:, pl.ds(pl.multiple_of((8 * zlo + 2 * g) * 128, 256), 256)]

    def give(g):
        return remote(result.at[1, g], columns(g), out_send.at[g], out_recv.at[g], pair)

    def keep_own(g):
        return pltpu.make_async_copy(result.at[0, g], columns(g), local_sem.at[5 + g])

    def attend(g):
        query_pair(g).wait_recv()
        when(run >= 1, next_run(g, 1).wait_recv)
        when(run >= 2, second_run(g).wait_recv)
        when(run >= 2, from_relay(g).wait_recv)

        def theirs(i, _):
            query_head(g, 1 - zlo, q_in[2 * g + i],
                       result.at[1, g, :, pl.ds(pl.multiple_of(i * 128, 128), 128)])
            return 0

        def ours(i, _):
            query_head(g, zlo, q_own[8 * zlo + 2 * g + i],
                       result.at[0, g, :, pl.ds(pl.multiple_of(i * 128, 128), 128)])
            return 0

        lax.fori_loop(0, 2, theirs, 0)
        give(g).start()
        lax.fori_loop(0, 2, ours, 0)
        keep_own(g).start()

    hop(0)
    hop(1)
    forward(0)
    send_own(2)
    hop(2)
    forward(1)
    send_own(3)
    attend(0)
    hop(3)
    forward(2)
    attend(1)
    forward(3)
    attend(2)
    attend(3)

    for copy in sent:
        copy.wait_send()

    def drain(h, _):
        part(h).wait_send()
        return 0

    lax.fori_loop(0, 16, drain, 0)
    for g in range(4):
        over_pair(g).wait_send()
        query_pair(g).wait_send()
        when(has_next, next_run(g, 0).wait_send)
        when(has_next, next_run(g, 1).wait_send)
        when((run >= 1) & has_next, second_run(g).wait_send)
        when(has_second, to_relay(g).wait_send)
        when(relays, from_relay(g).wait_send)
        keep_own(g).wait()
        give(g).wait()


def on_device(tokens, norm_gain, w_query, w_keyval, q_gain, k_gain):
    rows, width = tokens.shape[1:]
    quarter, cols = w_query.shape
    heads = cols * lax.axis_size("seq") // q_gain.shape[0]
    half = q_gain.shape[0] // 2
    third = quarter // 3
    shard = jnp.concatenate([w_query, w_keyval], axis=1).reshape(3, third, 2 * cols)
    place = (lax.axis_index("seq") * rows + jnp.arange(rows)).astype(F32)
    freq = jnp.power(10000.0, -2.0 * jnp.arange(half).astype(F32) / (2 * half))
    angle = place[:, None] * freq[None, :]
    cos = jnp.tile(jnp.cos(angle), (1, 2))
    sin = jnp.tile(jnp.sin(angle), (1, 2))
    ga = jnp.concatenate([q_gain[:half], k_gain[:half]])[None]
    gb = jnp.concatenate([q_gain[half:], k_gain[half:]])[None]
    vmem = pl.BlockSpec(memory_space=pltpu.VMEM)
    anyspace = pl.BlockSpec(memory_space=pl.ANY)
    dma = pltpu.SemaphoreType.DMA
    block = pltpu.VMEM((4, 4, 4, third, 128), BF16)
    out = pl.pallas_call(
        layer_kernel,
        name="layer",
        out_shape=jax.ShapeDtypeStruct((rows, heads * 128), BF16),
        in_specs=[vmem, vmem, anyspace, vmem, vmem, vmem, vmem],
        out_specs=vmem,
        scratch_shapes=[
            block, block, block,
            pltpu.VMEM((4, 3, rows, third), BF16),
            pltpu.VMEM((2, 2, 3, rows, third), BF16),
            pltpu.VMEM((heads, 2, rows, 256), F32),
            pltpu.VMEM((heads, rows, 256), F32),
            pltpu.VMEM((heads, rows, 256), BF16),
            pltpu.VMEM((heads // 2, rows, 256), BF16),
            pltpu.VMEM((4, rows, 384), BF16),
            pltpu.VMEM((4, 6, rows, 384), BF16),
            pltpu.VMEM((4, rows, 384), BF16),
            pltpu.VMEM((2, 4, rows, 256), BF16),
            dma((9,)), dma((3, 3, 2, 2)), dma((3, 3, 2, 2)),
            dma((2,)), dma((2,)), dma((heads,)), dma((heads,)),
            dma((2, 4)), dma((2, 4)), dma((5, 4)), dma((4, 4)), dma((4,)),
            dma((4,)), dma((4,)),
        ],
        compiler_params=pltpu.CompilerParams(
            collective_id=0, has_side_effects=True, vmem_limit_bytes=67043328),
    )(tokens[0], norm_gain[None], shard, cos, sin, ga, gb)
    return out[None]


def solution(mesh):
    in_specs = (P("fsdp", "seq", None), P(), P("fsdp", "seq"), P("fsdp", "seq"), P(), P())
    out_specs = P("fsdp", "seq", None)
    return jax.shard_map(
        on_device, mesh=mesh, in_specs=in_specs, out_specs=out_specs, check_vma=False
    )
```

```python
import functools
import math

import jax
import jax.numpy as jnp
from jax import lax
from jax.experimental import pallas as pl
from jax.experimental.pallas import tpu as pltpu
from jax.sharding import PartitionSpec as P

WINDOW = 1024
QSCALE = 168
MESH = pl.DeviceIdType.MESH
F32 = jnp.float32
BF16 = jnp.bfloat16
NEG = -1e30

WIDTHS = (512, 512, 320)
STARTS = (0, 512, 1024)
ORDERS = {
    "kv": (("x", "y", "z"), ("y", "z", "x"), ("z", "x", "y")),
    "q": (("x", "z", "y"), ("x", "y", "z"), ("x", "z", "y")),
}


def position():
    f, s = lax.axis_index("fsdp"), lax.axis_index("seq")
    return {"x": (s // 2) % 4, "y": s // 8, "z": 2 * (f // 2) + s % 2}, f % 2


def device(at, core):
    return (2 * (at["z"] // 2) + core, 8 * at["y"] + 2 * at["x"] + at["z"] % 2)


def shifted(at, dim, by):
    moved = dict(at)
    moved[dim] = (at[dim] + by + 4) % 4
    return moved


def layer_kernel(
    tok_hbm, gain_ref, wq_ref, wkv_ref, cos_hbm, sin_hbm, qg_ref, kg_ref,
    out_ref,
    kv0, kv1, kv2, q0, q1, q2, tok, cos_ref, sin_ref,
    normed, spread, acc, other, q_own, q_in, kv_out, kv, relay, result,
    local_sem, ring_send, ring_recv, tok_send, tok_recv, part_send, part_recv,
    pair_send, pair_recv, x_send, x_recv, relay_recv, out_send, out_recv,
):
    at, core = position()
    partner = device(at, 1 - core)
    rows, quarter = tok.shape[0], wq_ref.shape[1]
    weights = {"kv": (kv0, kv1, kv2), "q": (q0, q1, q2)}
    shards = {"kv": wkv_ref, "q": wq_ref}
    kinds = ("kv", "q")
    f, s = lax.axis_index("fsdp"), lax.axis_index("seq")
    zlo = s % 2
    run = s // 2
    runs = 16

    relayed = 4 * at["y"] + (at["x"] + 1) % 4
    relay_to = (f, 2 * ((relayed + 2) % runs) + zlo)
    relay_by = device(shifted(at, "x", -1), core)
    ahead = (f, (s + 2) % (2 * runs))
    behind = (f, (s - 2 + 2 * runs) % (2 * runs))
    pair = (f, s + 1 - 2 * zlo)
    source = (run - 2 + runs) % runs
    relay_from = (f, 2 * (4 * (source // 4) + (source + 3) % 4) + zlo)

    barrier = pltpu.get_barrier_semaphore()
    peers = [device(shifted(at, d, by), core) for d in "xyz" for by in (1, -1)]
    peers += [partner, ahead, behind, relay_to, relay_from]
    for peer in peers:
        pl.semaphore_signal(barrier, inc=1, device_id=peer, device_id_type=MESH)

    def clear(first, absent):
        @pl.when(absent)
        def _():
            kv[:, first:first + 2] = jnp.zeros((4, 2) + kv.shape[2:], BF16)

    clear(0, run < 2)
    clear(2, run < 1)

    fetched = [
        pltpu.make_async_copy(tok_hbm, tok, local_sem.at[9]),
        pltpu.make_async_copy(cos_hbm, cos_ref, local_sem.at[10]),
        pltpu.make_async_copy(sin_hbm, sin_ref, local_sem.at[11]),
    ]
    for copy in fetched:
        copy.start()
    for kind in kinds:
        for c, (d1, d2, d3) in enumerate(ORDERS[kind]):
            weights[kind][c][at[d3], at[d2], at[d1]] = (
                shards[kind][:, STARTS[c]:STARTS[c] + WIDTHS[c]])
    pl.semaphore_wait(barrier, len(peers))

    sent = []

    def view(kind, c, phase, index, half):
        d1, d2, d3 = ORDERS[kind][c]
        w = weights[kind][c]
        if phase == 0:
            if half is None:
                return w.at[at[d3], at[d2], index]
            return w.at[at[d3], at[d2], index, pl.ds(32 * half, 32)]
        if phase == 1:
            if half is None:
                return w.at[at[d3], index]
            return w.at[at[d3], index, pl.ds(2 * half, 2)]
        if half is None:
            return w.at[index]
        return w.at[index, pl.ds(2 * half, 2)]

    def ring(kind, c, phase, step):
        dim = ORDERS[kind][c][phase]
        copies = []
        for side, by in enumerate((1, -1)):
            if step == 0:
                block = view(kind, c, phase, at[dim], None)
            else:
                block = view(kind, c, phase, shifted(at, dim, -by)[dim], side)
            where = (kinds.index(kind), c, phase, step, side)
            copies.append(pltpu.make_async_remote_copy(
                src_ref=block, dst_ref=block,
                send_sem=ring_send.at[where], recv_sem=ring_recv.at[where],
                device_id=device(shifted(at, dim, by), core), device_id_type=MESH))
        return copies

    flying = {}

    def start_ring(kind, phase, step):
        flying[kind] = [ring(kind, c, phase, step) for c in range(3)]
        for copies in flying[kind]:
            for copy in copies:
                copy.start()
            sent.extend(copies)

    def wait_ring(kind):
        for copies in flying[kind]:
            for copy in copies:
                copy.wait_recv()

    start_ring("kv", 0, 0)
    wait_ring("kv")
    start_ring("kv", 0, 1)
    start_ring("q", 0, 0)
    wait_ring("kv")
    start_ring("kv", 1, 0)
    wait_ring("q")
    start_ring("q", 0, 1)
    wait_ring("kv")
    start_ring("kv", 1, 1)
    wait_ring("kv")
    start_ring("kv", 2, 0)
    wait_ring("q")

    strip = 32
    for copy in fetched:
        copy.wait()
    gain = jnp.concatenate([gain_ref[j:j + 1] for j in range(gain_ref.shape[0])], axis=1)

    def norm_rows(i, _):
        at_row = pl.ds(pl.multiple_of(i * strip, strip), strip)
        flat = tok[at_row, :].astype(F32)
        mean = jnp.mean(flat * flat, axis=-1, keepdims=True)
        out = (flat * lax.rsqrt(mean + 1e-6) * gain).astype(BF16)
        for k in range(4):
            normed[k, at_row, :] = out[:, k * quarter:(k + 1) * quarter]
        return 0

    lax.fori_loop(0, rows // strip, norm_rows, 0)
    exchange = []
    for zh in range(2):
        pltpu_copy = pltpu.make_async_copy(
            normed.at[2 * zh + core], spread.at[zh, core], local_sem.at[3 + zh])
        pltpu_copy.start()
        remote = pltpu.make_async_remote_copy(
            src_ref=normed.at[2 * zh + 1 - core], dst_ref=spread.at[zh, core],
            send_sem=tok_send.at[zh], recv_sem=tok_recv.at[zh],
            device_id=partner, device_id_type=MESH)
        remote.start()
        exchange.append((pltpu_copy, remote))
    for mine, remote in exchange:
        mine.wait()
        remote.wait()

    x, y, zown = at["x"], at["y"], at["z"] // 2
    zfar, mine_x = 1 - zown, x // 2
    far_y, far_x = (y + 2) % 4, 1 - mine_x

    def weight(kind, c, z, yy, xx):
        index = {"x": xx, "y": yy, "z": z}
        d1, d2, d3 = ORDERS[kind][c]
        return weights[kind][c][index[d3], index[d2], index[d1]]

    def units(kind, yy, xp, parts, first):
        h = 8 * kinds.index(kind) + 2 * yy + xp
        total = None
        for c, zh in parts:
            rhs = jnp.concatenate(
                [weight(kind, c, 2 * zh + z, yy, 2 * xp + i) for i in (0, 1) for z in (0, 1)], axis=0)
            lhs = spread[zh, :, :, STARTS[c]:STARTS[c] + WIDTHS[c]].reshape(2 * rows, WIDTHS[c])
            term = lax.dot_general(lhs, rhs, (((1,), (1,)), ((), ())), preferred_element_type=F32)
            total = term if total is None else total + term
        total = total.reshape(2, rows, 256)
        if first:
            acc[h] = total
        else:
            acc[h] += total

    def part(h):
        return pltpu.make_async_remote_copy(
            src_ref=acc.at[h, 1 - core], dst_ref=other.at[h],
            send_sem=part_send.at[h], recv_sem=part_recv.at[h],
            device_id=partner, device_id_type=MESH)

    both = lambda c: [(c, 0), (c, 1)]

    def loop(n, body):
        def step(i, _):
            body(i)
            return 0
        lax.fori_loop(0, n, step, 0)

    def near(k):
        return (y + k + k // 2) % 4

    def early(kind, yy, xp, parts):
        units(kind, yy, xp, parts, True)

    def late(kind, yy, xp, parts):
        units(kind, yy, xp, parts, False)
        part(8 * kinds.index(kind) + 2 * yy + xp).start()

    wait_ring("kv")
    start_ring("kv", 2, 1)
    start_ring("q", 1, 0)
    loop(3, lambda i: early("kv", near(i), mine_x, [(0, zown)] + both(1) + both(2)))
    early("kv", far_y, mine_x, [(0, zown)] + both(1))
    loop(3, lambda i: early("kv", near(i), far_x, [(0, zown)] + both(2)))
    early("kv", far_y, far_x, [(0, zown)])
    wait_ring("kv")
    loop(3, lambda i: late("kv", near(i), mine_x, [(0, zfar)]))
    late("kv", far_y, mine_x, [(0, zfar)] + both(2))
    loop(3, lambda i: late("kv", near(i), far_x, [(0, zfar)] + both(1)))
    late("kv", far_y, far_x, [(0, zfar)] + both(1) + both(2))
    wait_ring("q")
    start_ring("q", 1, 1)

    def turned(values, gain):
        mean = jnp.mean(values * values, axis=-1, keepdims=True)
        values = values * lax.rsqrt(mean + 1e-6) * gain
        return values * cos_ref[...] + pltpu.roll(values, 64, 1) * sin_ref[...]

    def in_two(ref, values):
        high = values.astype(BF16)
        ref[:, 0:128] = high
        ref[:, 128:256] = (values - high.astype(F32)).astype(BF16)

    def summed(h, i):
        lanes = slice(128 * i, 128 * i + 128)
        return acc[h, core, :, lanes] + other[h, :, lanes]

    def remote(src, dst, send_sem, recv_sem, to):
        return pltpu.make_async_remote_copy(
            src_ref=src, dst_ref=dst, send_sem=send_sem, recv_sem=recv_sem,
            device_id=to, device_id_type=MESH)

    def over_pair(g):
        return remote(kv_out.at[g], kv.at[g, 4 + zlo], pair_send.at[0, g], pair_recv.at[0, g], pair)

    def query_pair(g):
        mine = pl.ds(8 * (1 - zlo) + 2 * g, 2)
        return remote(q_own.at[mine], q_in.at[pl.ds(2 * g, 2)],
                      pair_send.at[1, g], pair_recv.at[1, g], pair)

    def next_run(g, block):
        return remote(kv.at[g, 4 + block], kv.at[g, 2 + block],
                      x_send.at[block, g], x_recv.at[2 + block, g], ahead)

    def second_run(g):
        return remote(kv.at[g, 2], kv.at[g, 0], x_send.at[2, g], x_recv.at[0, g], ahead)

    def to_relay(g):
        return remote(kv.at[g, 5], relay.at[g], x_send.at[3, g], relay_recv.at[g], relay_by)

    def from_relay(g):
        return remote(relay.at[g], kv.at[g, 1], x_send.at[4, g], x_recv.at[1, g], relay_to)

    def when(condition, action):
        @pl.when(condition)
        def _():
            action()

    has_next, has_second = run + 1 < runs, run + 2 < runs
    relays = relayed + 2 < runs

    def send_own(g):
        when(has_next, next_run(g, zlo).start)
        when(has_second & (zlo == 1), to_relay(g).start)

    def hop(g):
        over_pair(g).wait_recv()
        when(has_next, next_run(g, 1 - zlo).start)
        when(has_second & (zlo == 0), to_relay(g).start)

    def forward(g):
        when(run >= 1, next_run(g, 0).wait_recv)
        when((run >= 1) & has_next, second_run(g).start)
        when(relays, to_relay(g).wait_recv)
        when(relays, from_relay(g).start)

    def key_values(j):
        for mine in (True, False):
            half = zlo if mine else 1 - zlo
            key_pair, value_pair = 2 * half + j, 4 + 2 * half + j
            part(key_pair).wait_recv()
            part(value_pair).wait_recv()
            for i in (0, 1):
                g = 2 * j + i
                keep = kv.at[g, 4 + zlo] if mine else kv_out.at[g]
                in_two(keep, turned(summed(key_pair, i), kg_ref[...]))
                keep[:, 256:384] = summed(value_pair, i).astype(BF16)
        over_pair(2 * j).start()
        over_pair(2 * j + 1).start()
        when(j == 0, lambda: send_own(0))
        when(j == 0, lambda: send_own(1))

    loop(2, key_values)
    wait_ring("q")
    start_ring("q", 2, 0)
    hop(0)
    hop(1)
    forward(0)
    send_own(2)
    hop(2)
    forward(1)
    send_own(3)
    hop(3)
    forward(2)
    wait_ring("q")
    start_ring("q", 2, 1)
    forward(3)

    loop(6, lambda i: early("q", near(i // 2), i % 2, [(1, zown)] + both(0) + both(2)))
    loop(2, lambda i: early("q", far_y, i, [(1, zown)]))
    wait_ring("q")
    loop(6, lambda i: late("q", near(i // 2), i % 2, [(1, zfar)]))
    loop(2, lambda i: late("q", far_y, i, [(1, zfar)] + both(0) + both(2)))

    query_gain = qg_ref[...] * (QSCALE ** -0.5 * math.log2(math.e))

    def queries(g, mine):
        head = 8 * (zlo if mine else 1 - zlo) + 2 * g
        pair_unit = 8 + head // 2
        part(pair_unit).wait_recv()
        for i in (0, 1):
            in_two(q_own.at[head + i], turned(summed(pair_unit, i), query_gain))

    def theirs_first(g):
        queries(g, False)
        query_pair(g).start()

    loop(4, theirs_first)
    loop(4, lambda g: queries(g, True))

    row = lax.broadcasted_iota(jnp.int32, (2 * rows, rows), 0) % rows
    col = lax.broadcasted_iota(jnp.int32, (2 * rows, rows), 1)
    causal = col <= row

    def two_heads(g, token_block, q, keep):
        q = q.reshape(2 * rows, 256)
        q_hi, q_lo = q[:, 0:128], q[:, 128:256]
        q = jnp.concatenate([q_hi, q_hi, q_lo, q_lo], axis=1)
        pen = [jnp.where(2 * run - 4 + token_block + m >= 0, 0.0, NEG).astype(F32)
               for m in range(5)]

        def score(m):
            keys = kv[g, token_block + m, :, 0:256]
            keys = jnp.concatenate([keys, keys], axis=1)
            return lax.dot_general(q, keys, (((1,), (1,)), ((), ())), preferred_element_type=F32)

        edge = jnp.where(causal, score(4), score(0) + pen[0])
        inner = {m: score(m) for m in (1, 2, 3)}
        top = jnp.max(edge, axis=-1, keepdims=True)
        for m in inner:
            top = jnp.maximum(top, jnp.max(inner[m], axis=-1, keepdims=True) + pen[m])
        w_edge = jnp.exp2(edge - top)
        w_inner = {m: jnp.exp2(inner[m] - (top - pen[m])) for m in inner}
        total = jnp.sum(w_edge, axis=-1, keepdims=True)
        for m in inner:
            total = total + jnp.sum(w_inner[m], axis=-1, keepdims=True)
        inv = 1.0 / total
        p_edge = w_edge * inv
        probs = [jnp.where(causal, 0.0, p_edge)] + [w_inner[m] * inv for m in inner]
        probs.append(jnp.where(causal, p_edge, 0.0))
        probs = jnp.concatenate([p.astype(BF16) for p in probs], axis=1)
        values = kv[g, pl.ds(token_block, 5), :, 256:384].reshape(5 * rows, 128)
        out = jnp.dot(probs, values, preferred_element_type=F32).astype(BF16)
        keep[:, 0:128] = out[:rows]
        keep[:, 128:256] = out[rows:]

    def columns(g):
        return out_ref.at[:, pl.ds(pl.multiple_of((8 * zlo + 2 * g) * 128, 256), 256)]

    def give(g):
        return remote(result.at[1, g], columns(g), out_send.at[g], out_recv.at[g], pair)

    def keep_own(g):
        return pltpu.make_async_copy(result.at[0, g], columns(g), local_sem.at[5 + g])

    def mine_of(g):
        when(run >= 1, next_run(g, 1).wait_recv)
        when(run >= 2, second_run(g).wait_recv)
        when(run >= 2, from_relay(g).wait_recv)
        two_heads(g, zlo, q_own[pl.ds(8 * zlo + 2 * g, 2)], result.at[0, g])
        keep_own(g).start()

    def theirs_of(g):
        query_pair(g).wait_recv()
        two_heads(g, 1 - zlo, q_in[pl.ds(2 * g, 2)], result.at[1, g])
        give(g).start()

    loop(4, mine_of)
    loop(4, theirs_of)

    for copy in sent:
        copy.wait_send()

    def drain(h, _):
        part(h).wait_send()
        return 0

    lax.fori_loop(0, 16, drain, 0)
    for g in range(4):
        over_pair(g).wait_send()
        query_pair(g).wait_send()
        when(has_next, next_run(g, 0).wait_send)
        when(has_next, next_run(g, 1).wait_send)
        when((run >= 1) & has_next, second_run(g).wait_send)
        when(has_second, to_relay(g).wait_send)
        when(relays, from_relay(g).wait_send)
        keep_own(g).wait()
        give(g).wait()


def on_device(tokens, norm_gain, w_query, w_keyval, q_gain, k_gain):
    rows, width = tokens.shape[1:]
    quarter, cols = w_query.shape
    heads = cols * lax.axis_size("seq") // q_gain.shape[0]
    half = q_gain.shape[0] // 2
    place = (lax.axis_index("seq") * rows + jnp.arange(rows)).astype(F32)
    freq = jnp.power(10000.0, -2.0 * (jnp.arange(2 * half) % half).astype(F32) / (2 * half))
    angle = place[:, None] * freq[None, :]
    cos = jnp.cos(angle)
    sin = jnp.where(jnp.arange(2 * half) < half, -1.0, 1.0) * jnp.sin(angle)
    vmem = pl.BlockSpec(memory_space=pltpu.VMEM)
    anyspace = pl.BlockSpec(memory_space=pl.ANY)
    dma = pltpu.SemaphoreType.DMA
    blocks = [pltpu.VMEM((4, 4, 4, cols, width), BF16) for width in WIDTHS]
    out = pl.pallas_call(
        layer_kernel,
        name="layer",
        out_shape=jax.ShapeDtypeStruct((rows, heads * 128), BF16),
        in_specs=[anyspace, vmem, vmem, vmem, anyspace, anyspace, vmem, vmem],
        out_specs=vmem,
        scratch_shapes=[
            *blocks, *blocks,
            pltpu.VMEM((rows, width), BF16),
            pltpu.VMEM((rows, 128), F32),
            pltpu.VMEM((rows, 128), F32),
            pltpu.VMEM((4, rows, quarter), BF16),
            pltpu.VMEM((2, 2, rows, quarter), BF16),
            pltpu.VMEM((heads, 2, rows, 256), F32),
            pltpu.VMEM((heads, rows, 256), F32),
            pltpu.VMEM((heads, rows, 256), BF16),
            pltpu.VMEM((heads // 2, rows, 256), BF16),
            pltpu.VMEM((4, rows, 384), BF16),
            pltpu.VMEM((4, 6, rows, 384), BF16),
            pltpu.VMEM((4, rows, 384), BF16),
            pltpu.VMEM((2, 4, rows, 256), BF16),
            dma((12,)), dma((2, 3, 3, 2, 2)), dma((2, 3, 3, 2, 2)),
            dma((2,)), dma((2,)), dma((heads,)), dma((heads,)),
            dma((2, 4)), dma((2, 4)), dma((5, 4)), dma((4, 4)), dma((4,)),
            dma((4,)), dma((4,)),
        ],
        compiler_params=pltpu.CompilerParams(
            collective_id=0, has_side_effects=True, vmem_limit_bytes=67043328),
    )(tokens[0], norm_gain.reshape(-1, 128), w_query.T, w_keyval.T, cos, sin,
      q_gain[None], k_gain[None])
    return out[None]


def solution(mesh):
    in_specs = (P("fsdp", "seq", None), P(), P("fsdp", "seq"), P("fsdp", "seq"), P(), P())
    out_specs = P("fsdp", "seq", None)
    return jax.shard_map(
        on_device, mesh=mesh, in_specs=in_specs, out_specs=out_specs, check_vma=False
    )
```

```python
import functools
import math

import jax
import jax.numpy as jnp
from jax import lax
from jax.experimental import pallas as pl
from jax.experimental.pallas import tpu as pltpu
from jax.sharding import PartitionSpec as P

WINDOW = 1024
QSCALE = 168
MESH = pl.DeviceIdType.MESH
F32 = jnp.float32
BF16 = jnp.bfloat16
NEG = -1e30

ORDERS = (("x", "y", "z"), ("y", "z", "x"), ("z", "x", "y"))


def position():
    f, s = lax.axis_index("fsdp"), lax.axis_index("seq")
    return {"x": (s // 2) % 4, "y": s // 8, "z": 2 * (f // 2) + s % 2}, f % 2


def device(at, core):
    return (2 * (at["z"] // 2) + core, 8 * at["y"] + 2 * at["x"] + at["z"] % 2)


def shifted(at, dim, by):
    moved = dict(at)
    moved[dim] = (at[dim] + by + 4) % 4
    return moved


def layer_kernel(
    tok_hbm, gain_ref, shard_hbm, cos_hbm, sin_hbm, qg_ref, kg_ref,
    out_ref,
    w0, w1, w2, tok, cos_ref, sin_ref,
    normed, spread, acc, other, q_own, q_in, kv_out, kv, relay, result,
    local_sem, ring_send, ring_recv, tok_send, tok_recv, part_send, part_recv,
    pair_send, pair_recv, x_send, x_recv, relay_recv, out_send, out_recv,
):
    at, core = position()
    partner = device(at, 1 - core)
    rows, third = tok.shape[0], w0.shape[3]
    weights = (w0, w1, w2)
    f, s = lax.axis_index("fsdp"), lax.axis_index("seq")
    zlo = s % 2
    run = s // 2
    runs = 16

    relayed = 4 * at["y"] + (at["x"] + 1) % 4
    relay_to = (f, 2 * ((relayed + 2) % runs) + zlo)
    relay_by = device(shifted(at, "x", -1), core)
    ahead = (f, (s + 2) % (2 * runs))
    behind = (f, (s - 2 + 2 * runs) % (2 * runs))
    pair = (f, s + 1 - 2 * zlo)
    source = (run - 2 + runs) % runs
    relay_from = (f, 2 * (4 * (source // 4) + (source + 3) % 4) + zlo)

    barrier = pltpu.get_barrier_semaphore()
    peers = [device(shifted(at, d, by), core) for d in "xyz" for by in (1, -1)]
    peers += [partner, ahead, behind, relay_to, relay_from]
    for peer in peers:
        pl.semaphore_signal(barrier, inc=1, device_id=peer, device_id_type=MESH)

    def clear(first, absent):
        @pl.when(absent)
        def _():
            kv[:, first:first + 2] = jnp.zeros((4, 2) + kv.shape[2:], BF16)

    clear(0, run < 2)
    clear(2, run < 1)

    fetched = [
        pltpu.make_async_copy(tok_hbm, tok, local_sem.at[9]),
        pltpu.make_async_copy(cos_hbm, cos_ref, local_sem.at[10]),
        pltpu.make_async_copy(sin_hbm, sin_ref, local_sem.at[11]),
    ]
    for copy in fetched:
        copy.start()
    own = []
    for c, (d1, d2, d3) in enumerate(ORDERS):
        own.append(pltpu.make_async_copy(
            shard_hbm.at[c], weights[c].at[at[d3], at[d2], at[d1]], local_sem.at[c]))
        own[-1].start()
    for copy in own:
        copy.wait()
    pl.semaphore_wait(barrier, len(peers))

    sent = []

    def view(c, phase, index, half):
        d1, d2, d3 = ORDERS[c]
        w = weights[c]
        if phase == 0:
            if half is None:
                return w.at[at[d3], at[d2], index]
            return w.at[at[d3], at[d2], index, pl.ds(half * (third // 2), third // 2)]
        if phase == 1:
            if half is None:
                return w.at[at[d3], index]
            return w.at[at[d3], index, pl.ds(2 * half, 2)]
        if half is None:
            return w.at[index]
        return w.at[index, pl.ds(2 * half, 2)]

    def ring(c, phase, step):
        dim = ORDERS[c][phase]
        copies = []
        for side, by in enumerate((1, -1)):
            if step == 0:
                block = view(c, phase, at[dim], None)
            else:
                block = view(c, phase, shifted(at, dim, -by)[dim], side)
            copies.append(pltpu.make_async_remote_copy(
                src_ref=block, dst_ref=block,
                send_sem=ring_send.at[c, phase, step, side],
                recv_sem=ring_recv.at[c, phase, step, side],
                device_id=device(shifted(at, dim, by), core), device_id_type=MESH))
        return copies

    def start(copies):
        for copy in copies:
            copy.start()
        sent.extend(copies)

    flying = [ring(c, 0, 0) for c in range(3)]
    for copies in flying:
        start(copies)

    def step_ring(phase, step):
        for c in range(3):
            for copy in flying[c]:
                copy.wait_recv()
            flying[c] = ring(c, phase, step)
            start(flying[c])

    for phase, step in ((0, 1), (1, 0), (1, 1), (2, 0)):
        step_ring(phase, step)

    strip = 32
    for copy in fetched:
        copy.wait()
    gain = jnp.concatenate([gain_ref[j:j + 1] for j in range(gain_ref.shape[0])], axis=1)

    def norm_rows(i, _):
        at_row = pl.ds(pl.multiple_of(i * strip, strip), strip)
        flat = tok[at_row, :].astype(F32)
        mean = jnp.mean(flat * flat, axis=-1, keepdims=True)
        out = (flat * lax.rsqrt(mean + 1e-6) * gain).astype(BF16)
        for k in range(4):
            for c in range(3):
                j = 3 * k + c
                normed[k, c, at_row, :] = out[:, j * third:(j + 1) * third]
        return 0

    lax.fori_loop(0, rows // strip, norm_rows, 0)
    exchange = []
    for zh in range(2):
        pltpu_copy = pltpu.make_async_copy(
            normed.at[2 * zh + core], spread.at[zh, core], local_sem.at[3 + zh])
        pltpu_copy.start()
        remote = pltpu.make_async_remote_copy(
            src_ref=normed.at[2 * zh + 1 - core], dst_ref=spread.at[zh, core],
            send_sem=tok_send.at[zh], recv_sem=tok_recv.at[zh],
            device_id=partner, device_id_type=MESH)
        remote.start()
        exchange.append((pltpu_copy, remote))
    for mine, remote in exchange:
        mine.wait()
        remote.wait()

    x, y, zown = at["x"], at["y"], at["z"] // 2
    zfar, far_x, far_y = 1 - zown, (x + 2) % 4, (y + 2) % 4

    def weight(c, z, yy, xx):
        index = {"x": xx, "y": yy, "z": z}
        d1, d2, d3 = ORDERS[c]
        return weights[c][index[d3], index[d2], index[d1]]

    def units(yy, xx, parts, first):
        h = 4 * yy + xx
        total = None
        for c, zh in parts:
            rhs = jnp.concatenate(
                [weight(c, 2 * zh, yy, xx), weight(c, 2 * zh + 1, yy, xx)], axis=1)
            term = jnp.dot(spread[zh, :, c].reshape(2 * rows, third), rhs,
                           preferred_element_type=F32)
            total = term if total is None else total + term
        total = total.reshape(2, rows, 256)
        if first:
            acc[h] = total
        else:
            acc[h] += total

    def part(h):
        return pltpu.make_async_remote_copy(
            src_ref=acc.at[h, 1 - core], dst_ref=other.at[h],
            send_sem=part_send.at[h], recv_sem=part_recv.at[h],
            device_id=partner, device_id_type=MESH)

    both = lambda c: [(c, 0), (c, 1)]

    def loop(n, body):
        def step(i, _):
            body(i)
            return 0
        lax.fori_loop(0, n, step, 0)

    def near(at_dim, k):
        return (at_dim + k + k // 2) % 4

    def late(yy, xx, parts):
        units(yy, xx, parts, False)
        part(4 * yy + xx).start()

    step_ring(2, 1)
    loop(9, lambda i: units(near(y, i // 3), near(x, i % 3), [(0, zown)] + both(1) + both(2), True))
    loop(3, lambda i: units(near(y, i), far_x, [(0, zown)] + both(2), True))
    loop(3, lambda i: units(far_y, near(x, i), [(0, zown)] + both(1), True))
    units(far_y, far_x, [(0, zown)], True)
    for copies in flying:
        for copy in copies:
            copy.wait_recv()

    def late_group(g):
        @pl.when(g != far_x)
        def _():
            loop(3, lambda i: late(near(y, i), g, [(0, zfar)]))
            late(far_y, g, [(0, zfar)] + both(2))

        @pl.when(g == far_x)
        def _():
            loop(3, lambda i: late(near(y, i), g, [(0, zfar)] + both(1)))
            late(far_y, g, [(0, zfar)] + both(1) + both(2))

    def turned(values, gain):
        mean = jnp.mean(values * values, axis=-1, keepdims=True)
        values = values * lax.rsqrt(mean + 1e-6) * gain
        return values * cos_ref[...] + pltpu.roll(values, 64, 1) * sin_ref[...]

    def in_two(ref, values):
        high = values.astype(BF16)
        ref[:, 0:128] = high
        ref[:, 128:256] = (values - high.astype(F32)).astype(BF16)

    low = lax.broadcasted_iota(jnp.int32, (rows, 128), 1) < 64

    def summed(h, is_query):
        first = acc[h, core, :, 0:128] + other[h, :, 0:128]
        second = acc[h, core, :, 128:256] + other[h, :, 128:256]
        if is_query:
            return jnp.where(low, first, pltpu.roll(second, 64, 1))
        return jnp.where(low, pltpu.roll(first, 64, 1), second)

    def remote(src, dst, send_sem, recv_sem, to):
        return pltpu.make_async_remote_copy(
            src_ref=src, dst_ref=dst, send_sem=send_sem, recv_sem=recv_sem,
            device_id=to, device_id_type=MESH)

    def over_pair(g):
        return remote(kv_out.at[g], kv.at[g, 4 + zlo], pair_send.at[0, g], pair_recv.at[0, g], pair)

    def query_pair(g):
        mine = pl.ds(8 * (1 - zlo) + 2 * g, 2)
        return remote(q_own.at[mine], q_in.at[pl.ds(2 * g, 2)],
                      pair_send.at[1, g], pair_recv.at[1, g], pair)

    def next_run(g, block):
        return remote(kv.at[g, 4 + block], kv.at[g, 2 + block],
                      x_send.at[block, g], x_recv.at[2 + block, g], ahead)

    def second_run(g):
        return remote(kv.at[g, 2], kv.at[g, 0], x_send.at[2, g], x_recv.at[0, g], ahead)

    def to_relay(g):
        return remote(kv.at[g, 5], relay.at[g], x_send.at[3, g], relay_recv.at[g], relay_by)

    def from_relay(g):
        return remote(relay.at[g], kv.at[g, 1], x_send.at[4, g], x_recv.at[1, g], relay_to)

    def when(condition, action):
        @pl.when(condition)
        def _():
            action()

    has_next, has_second = run + 1 < runs, run + 2 < runs
    relays = relayed + 2 < runs

    def send_own(g):
        when(has_next, next_run(g, zlo).start)
        when(has_second & (zlo == 1), to_relay(g).start)

    def hop(g):
        over_pair(g).wait_recv()
        when(has_next, next_run(g, 1 - zlo).start)
        when(has_second & (zlo == 0), to_relay(g).start)

    def forward(g):
        when(run >= 1, next_run(g, 0).wait_recv)
        when((run >= 1) & has_next, second_run(g).start)
        when(relays, to_relay(g).wait_recv)
        when(relays, from_relay(g).start)

    def key_values(g):
        for mine in (True, False):
            k = 4 * (zlo if mine else 1 - zlo) + g
            keep = kv.at[g, 4 + zlo] if mine else kv_out.at[g]
            part(k).wait_recv()
            part(8 + k).wait_recv()
            in_two(keep, turned(summed(k, False), kg_ref[...]))
            keep[:, 256:384] = summed(8 + k, False).astype(BF16)
        over_pair(g).start()
        when(g < 2, lambda: send_own(g))

    def stage(n):
        when(n < 4, lambda: late_group(n))
        when(n > 0, lambda: key_values(n - 1))

    loop(5, stage)

    query_gain = qg_ref[...] * (QSCALE ** -0.5 * math.log2(math.e))

    def queries(g, mine):
        head = 8 * (zlo if mine else 1 - zlo) + 2 * g
        for i in (0, 1):
            in_two(q_own.at[head + i], turned(summed(head + i, True), query_gain))

    def queries_out(g):
        queries(g, False)
        query_pair(g).start()

    hop(0)
    hop(1)
    loop(4, queries_out)
    forward(0)
    send_own(2)
    hop(2)
    loop(4, lambda g: queries(g, True))

    row = lax.broadcasted_iota(jnp.int32, (2 * rows, rows), 0) % rows
    col = lax.broadcasted_iota(jnp.int32, (2 * rows, rows), 1)
    causal = col <= row

    def two_heads(g, token_block, q, keep):
        q = q.reshape(2 * rows, 256)
        q_hi, q_lo = q[:, 0:128], q[:, 128:256]
        q = jnp.concatenate([q_hi, q_hi, q_lo, q_lo], axis=1)
        pen = [jnp.where(2 * run - 4 + token_block + m >= 0, 0.0, NEG).astype(F32)
               for m in range(5)]

        def score(m):
            keys = kv[g, token_block + m, :, 0:256]
            keys = jnp.concatenate([keys, keys], axis=1)
            return lax.dot_general(q, keys, (((1,), (1,)), ((), ())), preferred_element_type=F32)

        edge = jnp.where(causal, score(4), score(0) + pen[0])
        inner = {m: score(m) for m in (1, 2, 3)}
        top = jnp.max(edge, axis=-1, keepdims=True)
        for m in inner:
            top = jnp.maximum(top, jnp.max(inner[m], axis=-1, keepdims=True) + pen[m])
        w_edge = jnp.exp2(edge - top)
        w_inner = {m: jnp.exp2(inner[m] - (top - pen[m])) for m in inner}
        total = jnp.sum(w_edge, axis=-1, keepdims=True)
        for m in inner:
            total = total + jnp.sum(w_inner[m], axis=-1, keepdims=True)
        inv = 1.0 / total
        p_edge = w_edge * inv
        probs = [jnp.where(causal, 0.0, p_edge)] + [w_inner[m] * inv for m in inner]
        probs.append(jnp.where(causal, p_edge, 0.0))
        probs = jnp.concatenate([p.astype(BF16) for p in probs], axis=1)
        values = kv[g, pl.ds(token_block, 5), :, 256:384].reshape(5 * rows, 128)
        out = jnp.dot(probs, values, preferred_element_type=F32).astype(BF16)
        keep[:, 0:128] = out[:rows]
        keep[:, 128:256] = out[rows:]

    def columns(g):
        return out_ref.at[:, pl.ds(pl.multiple_of((8 * zlo + 2 * g) * 128, 256), 256)]

    def give(g):
        return remote(result.at[1, g], columns(g), out_send.at[g], out_recv.at[g], pair)

    def keep_own(g):
        return pltpu.make_async_copy(result.at[0, g], columns(g), local_sem.at[5 + g])

    def mine_of(g):
        when(run >= 1, next_run(g, 1).wait_recv)
        when(run >= 2, second_run(g).wait_recv)
        when(run >= 2, from_relay(g).wait_recv)
        two_heads(g, zlo, q_own[pl.ds(8 * zlo + 2 * g, 2)], result.at[0, g])
        keep_own(g).start()

    def theirs_of(g):
        query_pair(g).wait_recv()
        two_heads(g, 1 - zlo, q_in[pl.ds(2 * g, 2)], result.at[1, g])
        give(g).start()

    def attend(g):
        mine_of(g)
        theirs_of(g)

    forward(1)
    send_own(3)
    attend(0)
    hop(3)
    forward(2)
    attend(1)
    forward(3)
    attend(2)
    attend(3)

    for copy in sent:
        copy.wait_send()

    def drain(h, _):
        part(h).wait_send()
        return 0

    lax.fori_loop(0, 16, drain, 0)
    for g in range(4):
        over_pair(g).wait_send()
        query_pair(g).wait_send()
        when(has_next, next_run(g, 0).wait_send)
        when(has_next, next_run(g, 1).wait_send)
        when((run >= 1) & has_next, second_run(g).wait_send)
        when(has_second, to_relay(g).wait_send)
        when(relays, from_relay(g).wait_send)
        keep_own(g).wait()
        give(g).wait()


def on_device(tokens, norm_gain, w_query, w_keyval, q_gain, k_gain):
    rows, width = tokens.shape[1:]
    quarter, cols = w_query.shape
    heads = cols * lax.axis_size("seq") // q_gain.shape[0]
    half = q_gain.shape[0] // 2
    third = quarter // 3
    shard = jnp.concatenate([w_query, w_keyval], axis=1).reshape(3, third, 2 * cols)
    place = (lax.axis_index("seq") * rows + jnp.arange(rows)).astype(F32)
    freq = jnp.power(10000.0, -2.0 * (jnp.arange(2 * half) % half).astype(F32) / (2 * half))
    angle = place[:, None] * freq[None, :]
    cos = jnp.cos(angle)
    sin = jnp.where(jnp.arange(2 * half) < half, -1.0, 1.0) * jnp.sin(angle)
    vmem = pl.BlockSpec(memory_space=pltpu.VMEM)
    anyspace = pl.BlockSpec(memory_space=pl.ANY)
    dma = pltpu.SemaphoreType.DMA
    block = pltpu.VMEM((4, 4, 4, third, 128), BF16)
    out = pl.pallas_call(
        layer_kernel,
        name="layer",
        out_shape=jax.ShapeDtypeStruct((rows, heads * 128), BF16),
        in_specs=[anyspace, vmem, anyspace, anyspace, anyspace, vmem, vmem],
        out_specs=vmem,
        scratch_shapes=[
            block, block, block,
            pltpu.VMEM((rows, width), BF16),
            pltpu.VMEM((rows, 128), F32),
            pltpu.VMEM((rows, 128), F32),
            pltpu.VMEM((4, 3, rows, third), BF16),
            pltpu.VMEM((2, 2, 3, rows, third), BF16),
            pltpu.VMEM((heads, 2, rows, 256), F32),
            pltpu.VMEM((heads, rows, 256), F32),
            pltpu.VMEM((heads, rows, 256), BF16),
            pltpu.VMEM((heads // 2, rows, 256), BF16),
            pltpu.VMEM((4, rows, 384), BF16),
            pltpu.VMEM((4, 6, rows, 384), BF16),
            pltpu.VMEM((4, rows, 384), BF16),
            pltpu.VMEM((2, 4, rows, 256), BF16),
            dma((12,)), dma((3, 3, 2, 2)), dma((3, 3, 2, 2)),
            dma((2,)), dma((2,)), dma((heads,)), dma((heads,)),
            dma((2, 4)), dma((2, 4)), dma((5, 4)), dma((4, 4)), dma((4,)),
            dma((4,)), dma((4,)),
        ],
        compiler_params=pltpu.CompilerParams(
            collective_id=0, has_side_effects=True, vmem_limit_bytes=67043328),
    )(tokens[0], norm_gain.reshape(-1, 128), shard, cos, sin,
      q_gain[None], k_gain[None])
    return out[None]


def solution(mesh):
    in_specs = (P("fsdp", "seq", None), P(), P("fsdp", "seq"), P("fsdp", "seq"), P(), P())
    out_specs = P("fsdp", "seq", None)
    return jax.shard_map(
        on_device, mesh=mesh, in_specs=in_specs, out_specs=out_specs, check_vma=False
    )
```

```python
import functools
import math

import jax
import jax.numpy as jnp
from jax import lax
from jax.experimental import pallas as pl
from jax.experimental.pallas import tpu as pltpu
from jax.sharding import PartitionSpec as P

WINDOW = 1024
QSCALE = 168
MESH = pl.DeviceIdType.MESH
F32 = jnp.float32
BF16 = jnp.bfloat16
NEG = -1e30

ORDERS = (("x", "y", "z"), ("y", "z", "x"), ("z", "x", "y"))


def position():
    f, s = lax.axis_index("fsdp"), lax.axis_index("seq")
    return {"x": (s // 2) % 4, "y": s // 8, "z": 2 * (f // 2) + s % 2}, f % 2


def device(at, core):
    return (2 * (at["z"] // 2) + core, 8 * at["y"] + 2 * at["x"] + at["z"] % 2)


def shifted(at, dim, by):
    moved = dict(at)
    moved[dim] = (at[dim] + by + 4) % 4
    return moved


def layer_kernel(
    tok_hbm, gain_ref, shard_hbm, cos_hbm, sin_hbm, qg_ref, kg_ref,
    out_ref,
    w0, w1, w2, tok, cos_ref, sin_ref,
    normed, spread, acc, top, other, q_own, q_in, kv_out, kv, relay, result,
    local_sem, ring_send, ring_recv, tok_send, tok_recv, part_send, part_recv,
    pair_send, pair_recv, x_send, x_recv, relay_recv, out_send, out_recv,
):
    at, core = position()
    partner = device(at, 1 - core)
    rows, third = tok.shape[0], w0.shape[3]
    weights = (w0, w1, w2)
    f, s = lax.axis_index("fsdp"), lax.axis_index("seq")
    zlo = s % 2
    run = s // 2
    runs = 16

    def on_row(xx, yy):
        return device({"x": (xx + 4) % 4, "y": (yy + 4) % 4, "z": at["z"]}, core)

    relay_by = on_row(at["x"] - 1, at["y"] + at["x"] // 2)
    source_x = (at["x"] + 1) % 4
    source_y = at["y"] - source_x // 2
    relay_from = on_row(source_x, source_y)
    relay_to = on_row(at["x"] - 1, at["y"])
    ahead = (f, (s + 2) % (2 * runs))
    behind = (f, (s - 2 + 2 * runs) % (2 * runs))
    pair = (f, s + 1 - 2 * zlo)

    barrier = pltpu.get_barrier_semaphore()
    peers = [device(shifted(at, d, by), core) for d in "xyz" for by in (1, -1)]
    peers += [partner, ahead, behind, relay_by, relay_from]
    for peer in peers:
        pl.semaphore_signal(barrier, inc=1, device_id=peer, device_id_type=MESH)

    def clear(first, absent):
        @pl.when(absent)
        def _():
            kv[:, first:first + 2] = jnp.zeros((4, 2) + kv.shape[2:], BF16)

    clear(0, run < 2)
    clear(2, run < 1)

    fetched = [
        pltpu.make_async_copy(tok_hbm, tok, local_sem.at[9]),
        pltpu.make_async_copy(cos_hbm, cos_ref, local_sem.at[10]),
        pltpu.make_async_copy(sin_hbm, sin_ref, local_sem.at[11]),
    ]
    for copy in fetched:
        copy.start()
    own = []
    for c, (d1, d2, d3) in enumerate(ORDERS):
        own.append(pltpu.make_async_copy(
            shard_hbm.at[c], weights[c].at[at[d3], at[d2], at[d1]], local_sem.at[c]))
        own[-1].start()
    for copy in own:
        copy.wait()
    pl.semaphore_wait(barrier, len(peers))

    sent = []

    def view(c, phase, index, half):
        d1, d2, d3 = ORDERS[c]
        w = weights[c]
        if phase == 0:
            if half is None:
                return w.at[at[d3], at[d2], index]
            return w.at[at[d3], at[d2], index, pl.ds(half * (third // 2), third // 2)]
        if phase == 1:
            if half is None:
                return w.at[at[d3], index]
            return w.at[at[d3], index, pl.ds(2 * half, 2)]
        if half is None:
            return w.at[index]
        return w.at[index, pl.ds(2 * half, 2)]

    def ring(c, phase, step):
        dim = ORDERS[c][phase]
        copies = []
        for side, by in enumerate((1, -1)):
            if step == 0:
                block = view(c, phase, at[dim], None)
            else:
                block = view(c, phase, shifted(at, dim, -by)[dim], side)
            copies.append(pltpu.make_async_remote_copy(
                src_ref=block, dst_ref=block,
                send_sem=ring_send.at[c, phase, step, side],
                recv_sem=ring_recv.at[c, phase, step, side],
                device_id=device(shifted(at, dim, by), core), device_id_type=MESH))
        return copies

    def start(copies):
        for copy in copies:
            copy.start()
        sent.extend(copies)

    flying = [ring(c, 0, 0) for c in range(3)]
    for copies in flying:
        start(copies)

    def step_ring(phase, step):
        for c in range(3):
            for copy in flying[c]:
                copy.wait_recv()
            flying[c] = ring(c, phase, step)
            start(flying[c])

    for phase, step in ((0, 1), (1, 0), (1, 1), (2, 0)):
        step_ring(phase, step)

    strip = 32
    for copy in fetched:
        copy.wait()
    gain = jnp.concatenate([gain_ref[j:j + 1] for j in range(gain_ref.shape[0])], axis=1)

    def norm_rows(i, _):
        at_row = pl.ds(pl.multiple_of(i * strip, strip), strip)
        flat = tok[at_row, :].astype(F32)
        mean = jnp.mean(flat * flat, axis=-1, keepdims=True)
        out = (flat * lax.rsqrt(mean + 1e-6) * gain).astype(BF16)
        for k in range(4):
            for c in range(3):
                j = 3 * k + c
                normed[k, c, at_row, :] = out[:, j * third:(j + 1) * third]
        return 0

    lax.fori_loop(0, rows // strip, norm_rows, 0)
    exchange = []
    for zh in range(2):
        pltpu_copy = pltpu.make_async_copy(
            normed.at[2 * zh + core], spread.at[zh, core], local_sem.at[3 + zh])
        pltpu_copy.start()
        remote = pltpu.make_async_remote_copy(
            src_ref=normed.at[2 * zh + 1 - core], dst_ref=spread.at[zh, core],
            send_sem=tok_send.at[zh], recv_sem=tok_recv.at[zh],
            device_id=partner, device_id_type=MESH)
        remote.start()
        exchange.append((pltpu_copy, remote))
    for mine, remote in exchange:
        mine.wait()
        remote.wait()

    x, y, zown = at["x"], at["y"], at["z"] // 2
    zfar, far_x, far_y = 1 - zown, (x + 2) % 4, (y + 2) % 4

    def weight(c, z, yy, xx):
        index = {"x": xx, "y": yy, "z": z}
        d1, d2, d3 = ORDERS[c]
        return weights[c][index[d3], index[d2], index[d1]]

    def units(yy, xx, parts, first):
        h = 4 * yy + xx
        total = None
        for c, zh in parts:
            rhs = jnp.concatenate(
                [weight(c, 2 * zh, yy, xx), weight(c, 2 * zh + 1, yy, xx)], axis=1)
            term = jnp.dot(spread[zh, :, c].reshape(2 * rows, third), rhs,
                           preferred_element_type=F32)
            total = term if total is None else total + term
        total = total.reshape(2, rows, 256)
        if first:
            acc[h] = total
        else:
            acc[h] += total

    def part(h):
        return pltpu.make_async_remote_copy(
            src_ref=acc.at[h, 1 - core], dst_ref=other.at[h],
            send_sem=part_send.at[h], recv_sem=part_recv.at[h],
            device_id=partner, device_id_type=MESH)

    both = lambda c: [(c, 0), (c, 1)]

    def loop(n, body):
        def step(i, _):
            body(i)
            return 0
        lax.fori_loop(0, n, step, 0)

    def near(at_dim, k):
        return (at_dim + k + k // 2) % 4

    def late(yy, xx, parts):
        units(yy, xx, parts, False)
        part(4 * yy + xx).start()

    step_ring(2, 1)
    loop(9, lambda i: units(near(y, i // 3), near(x, i % 3), [(0, zown)] + both(1) + both(2), True))
    loop(3, lambda i: units(near(y, i), far_x, [(0, zown)] + both(2), True))
    loop(3, lambda i: units(far_y, near(x, i), [(0, zown)] + both(1), True))
    units(far_y, far_x, [(0, zown)], True)
    for copies in flying:
        for copy in copies:
            copy.wait_recv()

    def late_group(g):
        @pl.when(g != far_x)
        def _():
            loop(3, lambda i: late(near(y, i), g, [(0, zfar)]))
            late(far_y, g, [(0, zfar)] + both(2))

        @pl.when(g == far_x)
        def _():
            loop(3, lambda i: late(near(y, i), g, [(0, zfar)] + both(1)))
            late(far_y, g, [(0, zfar)] + both(1) + both(2))

    def turned(values, gain):
        mean = jnp.mean(values * values, axis=-1, keepdims=True)
        values = values * lax.rsqrt(mean + 1e-6) * gain
        return values * cos_ref[...] + pltpu.roll(values, 64, 1) * sin_ref[...]

    def in_two(ref, values):
        high = values.astype(BF16)
        ref[:, 0:128] = high
        ref[:, 128:256] = (values - high.astype(F32)).astype(BF16)

    low = lax.broadcasted_iota(jnp.int32, (rows, 128), 1) < 64

    def summed(h, is_query):
        first = acc[h, core, :, 0:128] + other[h, :, 0:128]
        second = acc[h, core, :, 128:256] + other[h, :, 128:256]
        if is_query:
            return jnp.where(low, first, pltpu.roll(second, 64, 1))
        return jnp.where(low, pltpu.roll(first, 64, 1), second)

    def remote(src, dst, send_sem, recv_sem, to):
        return pltpu.make_async_remote_copy(
            src_ref=src, dst_ref=dst, send_sem=send_sem, recv_sem=recv_sem,
            device_id=to, device_id_type=MESH)

    def over_pair(g):
        return remote(kv_out.at[g], kv.at[g, 4 + zlo], pair_send.at[0, g], pair_recv.at[0, g], pair)

    def query_pair(g):
        mine = pl.ds(8 * (1 - zlo) + 2 * g, 2)
        return remote(q_own.at[mine], q_in.at[pl.ds(2 * g, 2)],
                      pair_send.at[1, g], pair_recv.at[1, g], pair)

    def next_run(g, block):
        return remote(kv.at[g, 4 + block], kv.at[g, 2 + block],
                      x_send.at[block, g], x_recv.at[2 + block, g], ahead)

    def second_run(g):
        return remote(kv.at[g, 2], kv.at[g, 0], x_send.at[2, g], x_recv.at[0, g], ahead)

    def to_relay(g):
        return remote(kv.at[g, 5], relay.at[g], x_send.at[3, g], relay_recv.at[g], relay_by)

    def from_relay(g):
        return remote(relay.at[g], kv.at[g, 1], x_send.at[4, g], x_recv.at[1, g], relay_to)

    def when(condition, action):
        @pl.when(condition)
        def _():
            action()

    has_next, has_second = run + 1 < runs, run + 2 < runs
    relays = source_y >= 0

    def send_own(g):
        when(has_next, next_run(g, zlo).start)
        when(has_second & (zlo == 1), to_relay(g).start)

    def hop(g):
        over_pair(g).wait_recv()
        when(has_next, next_run(g, 1 - zlo).start)
        when(has_second & (zlo == 0), to_relay(g).start)

    def forward(g):
        when(run >= 1, next_run(g, 0).wait_recv)
        when((run >= 1) & has_next, second_run(g).start)
        when(relays, to_relay(g).wait_recv)
        when(relays, from_relay(g).start)

    def key_values(g):
        for mine in (True, False):
            k = 4 * (zlo if mine else 1 - zlo) + g
            keep = kv.at[g, 4 + zlo] if mine else kv_out.at[g]
            part(k).wait_recv()
            part(8 + k).wait_recv()
            in_two(keep, turned(summed(k, False), kg_ref[...]))
            keep[:, 256:384] = summed(8 + k, False).astype(BF16)
        over_pair(g).start()
        when(g < 2, lambda: send_own(g))

    def stage(n):
        when(n < 4, lambda: late_group(n))
        when(n > 0, lambda: key_values(n - 1))

    loop(5, stage)

    query_gain = qg_ref[...] * (QSCALE ** -0.5 * math.log2(math.e))

    def queries(g, mine):
        head = 8 * (zlo if mine else 1 - zlo) + 2 * g
        for i in (0, 1):
            in_two(q_own.at[head + i], turned(summed(head + i, True), query_gain))

    def queries_out(g):
        queries(g, False)
        query_pair(g).start()

    hop(0)
    hop(1)
    loop(4, queries_out)
    forward(0)
    send_own(2)
    hop(2)
    hop(3)
    loop(4, lambda g: queries(g, True))
    loop(16, lambda h: part(h).wait_send())

    row = lax.broadcasted_iota(jnp.int32, (rows, rows), 0)
    col = lax.broadcasted_iota(jnp.int32, (rows, rows), 1)
    causal = col <= row

    def score_steps(slot, g, token_block, q):
        q = q.reshape(2 * rows, 256)
        q_hi, q_lo = q[:, 0:128], q[:, 128:256]
        q = jnp.concatenate([q_hi, q_hi, q_lo, q_lo], axis=1)
        pen = [jnp.where(2 * run - 4 + token_block + m >= 0, 0.0, NEG).astype(F32)
               for m in range(4)]
        best = []

        def score(m):
            keys = kv[g, token_block + m, :, 0:256]
            keys = jnp.concatenate([keys, keys], axis=1)
            out = lax.dot_general(q, keys, (((1,), (1,)), ((), ())), preferred_element_type=F32)
            return out.reshape(2, rows, 256)

        def tile(m):
            if m == 0:
                out = jnp.where(causal[None], score(4), score(0) + pen[0])
            else:
                out = score(m) + pen[m]
            acc[4 * slot + m] = out
            high = jnp.maximum(out[:, :, 0:128], out[:, :, 128:256])
            best.append(jnp.maximum(best[-1], high) if best else high)
            if m == 3:
                top[slot] = jnp.broadcast_to(
                    jnp.max(best[-1], axis=-1, keepdims=True), (2, rows, 128))

        return [functools.partial(tile, m) for m in range(4)]

    def value_steps(slot, g, token_block, keep):
        def one(i):
            high = top[slot, i, :, 0:1]
            w = [jnp.exp2(acc[4 * slot + m, i] - high) for m in range(4)]
            total = jnp.sum((w[0] + w[1]) + (w[2] + w[3]), axis=-1, keepdims=True)
            probs = [jnp.where(causal, 0.0, w[0]), w[1], w[2], w[3], jnp.where(causal, w[0], 0.0)]
            probs = jnp.concatenate([p.astype(BF16) for p in probs], axis=1)
            values = kv[g, pl.ds(token_block, 5), :, 256:384].reshape(5 * rows, 128)
            out = jnp.dot(probs, values, preferred_element_type=F32)
            keep[:, 128 * i:128 * i + 128] = (out * (1.0 / total)).astype(BF16)

        return [functools.partial(one, i) for i in (0, 1)]

    def columns(g):
        return out_ref.at[:, pl.ds(pl.multiple_of((8 * zlo + 2 * g) * 128, 256), 256)]

    def give(g):
        return remote(result.at[1, g], columns(g), out_send.at[g], out_recv.at[g], pair)

    def keep_own(g):
        return pltpu.make_async_copy(result.at[0, g], columns(g), local_sem.at[5 + g])

    def window(g):
        when(run >= 1, next_run(g, 1).wait_recv)
        when(run >= 2, second_run(g).wait_recv)
        when(run >= 2, from_relay(g).wait_recv)

    def score_mine(g):
        return score_steps(0, g, zlo, q_own[pl.ds(8 * zlo + 2 * g, 2)])

    def score_theirs(g):
        return score_steps(1, g, 1 - zlo, q_in[pl.ds(2 * g, 2)])

    def value_mine(g):
        return value_steps(0, g, zlo, result.at[0, g])

    def value_theirs(g):
        return value_steps(1, g, 1 - zlo, result.at[1, g])

    def together(scores, values):
        for n in (0, 4, 1, 2, 5, 3):
            steps = values if n >= 4 else scores
            if steps:
                steps[n % 4]()

    forward(1)
    send_own(3)
    window(0)
    together(score_mine(0), [])
    for g in range(4):
        query_pair(g).wait_recv()
        together(score_theirs(g), value_mine(g))
        keep_own(g).start()
        if g < 2:
            forward(g + 2)
        if g < 3:
            window(g + 1)
        together(score_mine(g + 1) if g < 3 else [], value_theirs(g))
        give(g).start()

    for copy in sent:
        copy.wait_send()

    for g in range(4):
        over_pair(g).wait_send()
        query_pair(g).wait_send()
        when(has_next, next_run(g, 0).wait_send)
        when(has_next, next_run(g, 1).wait_send)
        when((run >= 1) & has_next, second_run(g).wait_send)
        when(has_second, to_relay(g).wait_send)
        when(relays, from_relay(g).wait_send)
        keep_own(g).wait()
        give(g).wait()


def on_device(tokens, norm_gain, w_query, w_keyval, q_gain, k_gain):
    rows, width = tokens.shape[1:]
    quarter, cols = w_query.shape
    heads = cols * lax.axis_size("seq") // q_gain.shape[0]
    half = q_gain.shape[0] // 2
    third = quarter // 3
    shard = jnp.concatenate([w_query, w_keyval], axis=1).reshape(3, third, 2 * cols)
    place = (lax.axis_index("seq") * rows + jnp.arange(rows)).astype(F32)
    freq = jnp.power(10000.0, -2.0 * (jnp.arange(2 * half) % half).astype(F32) / (2 * half))
    angle = place[:, None] * freq[None, :]
    cos = jnp.cos(angle)
    sin = jnp.where(jnp.arange(2 * half) < half, -1.0, 1.0) * jnp.sin(angle)
    vmem = pl.BlockSpec(memory_space=pltpu.VMEM)
    anyspace = pl.BlockSpec(memory_space=pl.ANY)
    dma = pltpu.SemaphoreType.DMA
    block = pltpu.VMEM((4, 4, 4, third, 128), BF16)
    out = pl.pallas_call(
        layer_kernel,
        name="layer",
        out_shape=jax.ShapeDtypeStruct((rows, heads * 128), BF16),
        in_specs=[anyspace, vmem, anyspace, anyspace, anyspace, vmem, vmem],
        out_specs=vmem,
        scratch_shapes=[
            block, block, block,
            pltpu.VMEM((rows, width), BF16),
            pltpu.VMEM((rows, 128), F32),
            pltpu.VMEM((rows, 128), F32),
            pltpu.VMEM((4, 3, rows, third), BF16),
            pltpu.VMEM((2, 2, 3, rows, third), BF16),
            pltpu.VMEM((heads, 2, rows, 256), F32),
            pltpu.VMEM((2, 2, rows, 128), F32),
            pltpu.VMEM((heads, rows, 256), F32),
            pltpu.VMEM((heads, rows, 256), BF16),
            pltpu.VMEM((heads // 2, rows, 256), BF16),
            pltpu.VMEM((4, rows, 384), BF16),
            pltpu.VMEM((4, 6, rows, 384), BF16),
            pltpu.VMEM((4, rows, 384), BF16),
            pltpu.VMEM((2, 4, rows, 256), BF16),
            dma((12,)), dma((3, 3, 2, 2)), dma((3, 3, 2, 2)),
            dma((2,)), dma((2,)), dma((heads,)), dma((heads,)),
            dma((2, 4)), dma((2, 4)), dma((5, 4)), dma((4, 4)), dma((4,)),
            dma((4,)), dma((4,)),
        ],
        compiler_params=pltpu.CompilerParams(
            collective_id=0, has_side_effects=True, vmem_limit_bytes=62 * 2**20),
    )(tokens[0], norm_gain.reshape(-1, 128), shard, cos, sin,
      q_gain[None], k_gain[None])
    return out[None]


def solution(mesh):
    in_specs = (P("fsdp", "seq", None), P(), P("fsdp", "seq"), P("fsdp", "seq"), P(), P())
    out_specs = P("fsdp", "seq", None)
    return jax.shard_map(
        on_device, mesh=mesh, in_specs=in_specs, out_specs=out_specs, check_vma=False
    )
```

```python
import functools
import math

import jax
import jax.numpy as jnp
from jax import lax
from jax.experimental import pallas as pl
from jax.experimental.pallas import tpu as pltpu
from jax.sharding import PartitionSpec as P

WINDOW = 1024
QSCALE = 168
MESH = pl.DeviceIdType.MESH
F32 = jnp.float32
BF16 = jnp.bfloat16
NEG = -1e30
LAST = 3
STEP = 4

ORDERS = (("x", "y", "z"), ("y", "z", "x"), ("z", "x", "y"))


def position():
    f, s = lax.axis_index("fsdp"), lax.axis_index("seq")
    return {"x": (s // 2) % 4, "y": s // 8, "z": 2 * (f // 2) + s % 2}, f % 2


def device(at, core):
    return (2 * (at["z"] // 2) + core, 8 * at["y"] + 2 * at["x"] + at["z"] % 2)


def shifted(at, dim, by):
    moved = dict(at)
    moved[dim] = (at[dim] + by + 4) % 4
    return moved


def layer_kernel(
    tok_hbm, gain_ref, shard_hbm, cos_hbm, sin_hbm, qg_ref, kg_ref,
    out_ref,
    w0, w1, w2, tok, cos_ref, sin_ref,
    normed, spread, acc, top, other, q_own, q_in, kv_out, kv, relay, result,
    local_sem, ring_send, ring_recv, tok_send, tok_recv, part_send, part_recv,
    pair_send, pair_recv, x_send, x_recv, relay_recv, out_send, out_recv,
):
    at, core = position()
    partner = device(at, 1 - core)
    rows, third = tok.shape[0], w0.shape[3]
    weights = (w0, w1, w2)
    f, s = lax.axis_index("fsdp"), lax.axis_index("seq")
    zlo = s % 2
    run = s // 2
    runs = 16

    def on_row(xx, yy):
        return device({"x": (xx + 4) % 4, "y": (yy + 4) % 4, "z": at["z"]}, core)

    relay_by = on_row(at["x"] - 1, at["y"] + at["x"] // 2)
    source_x = (at["x"] + 1) % 4
    source_y = at["y"] - source_x // 2
    relay_from = on_row(source_x, source_y)
    relay_to = on_row(at["x"] - 1, at["y"])
    ahead = (f, (s + 2) % (2 * runs))
    behind = (f, (s - 2 + 2 * runs) % (2 * runs))
    pair = (f, s + 1 - 2 * zlo)

    barrier = pltpu.get_barrier_semaphore()
    peers = [device(shifted(at, d, by), core) for d in "xyz" for by in (1, -1)]
    peers += [partner, ahead, behind, relay_by, relay_from]
    for peer in peers:
        pl.semaphore_signal(barrier, inc=1, device_id=peer, device_id_type=MESH)

    def clear(first, absent):
        @pl.when(absent)
        def _():
            kv[:, first:first + 2] = jnp.zeros((4, 2) + kv.shape[2:], BF16)

    clear(0, run < 2)
    clear(2, run < 1)

    fetched = [
        pltpu.make_async_copy(tok_hbm, tok, local_sem.at[9]),
        pltpu.make_async_copy(cos_hbm, cos_ref, local_sem.at[10]),
        pltpu.make_async_copy(sin_hbm, sin_ref, local_sem.at[11]),
    ]
    for copy in fetched:
        copy.start()
    own = []
    for c, (d1, d2, d3) in enumerate(ORDERS):
        own.append(pltpu.make_async_copy(
            shard_hbm.at[c], weights[c].at[at[d3], at[d2], at[d1]], local_sem.at[c]))
        own[-1].start()
    for copy in own:
        copy.wait()
    pl.semaphore_wait(barrier, len(peers))

    sent = []

    def block(c, phase, index, part, half):
        d1, d2, d3 = ORDERS[c]
        w = weights[c]
        if phase == 0:
            if half is None:
                return w.at[at[d3], at[d2], index]
            return w.at[at[d3], at[d2], index, pl.ds(half * (third // 2), third // 2)]
        bundle = w.at[at[d3], index] if phase == 1 else w.at[index]
        if half is None:
            return bundle.at[(at[(d1, d2)[phase - 1]] + part) % 4]
        return bundle.at[pl.ds(2 * half, 2)]

    flying = {}

    def send(phase, *parts):
        for c in range(3):
            dim = ORDERS[c][phase]
            for part in parts:
                copies = []
                for side, by in enumerate((1, -1)):
                    if part == STEP:
                        ref = block(c, phase, shifted(at, dim, -by)[dim], None, side)
                    else:
                        ref = block(c, phase, at[dim], part, None)
                    copies.append(pltpu.make_async_remote_copy(
                        src_ref=ref, dst_ref=ref,
                        send_sem=ring_send.at[c, phase, part, side],
                        recv_sem=ring_recv.at[c, phase, part, side],
                        device_id=device(shifted(at, dim, by), core), device_id_type=MESH))
                    copies[-1].start()
                sent.extend(copies)
                flying[c, phase, part] = copies

    def receive(phase, *parts):
        for c in range(3):
            for part in parts:
                for copy in flying[c, phase, part]:
                    copy.wait_recv()

    send(0, 0)
    receive(0, 0)
    for phase in (0, 1):
        send(phase, STEP)
        send(phase + 1, 0, 1, 3)
        receive(phase, STEP)
        send(phase + 1, 2)
        if phase == 0:
            receive(1, 0, 1, 3, 2)

    strip = 32
    for copy in fetched:
        copy.wait()
    gain = jnp.concatenate([gain_ref[j:j + 1] for j in range(gain_ref.shape[0])], axis=1)

    def norm_rows(i, _):
        at_row = pl.ds(pl.multiple_of(i * strip, strip), strip)
        flat = tok[at_row, :].astype(F32)
        mean = jnp.mean(flat * flat, axis=-1, keepdims=True)
        out = (flat * lax.rsqrt(mean + 1e-6) * gain).astype(BF16)
        for k in range(4):
            for c in range(3):
                j = 3 * k + c
                normed[k, c, at_row, :] = out[:, j * third:(j + 1) * third]
        return 0

    lax.fori_loop(0, rows // strip, norm_rows, 0)
    exchange = []
    for zh in range(2):
        pltpu_copy = pltpu.make_async_copy(
            normed.at[2 * zh + core], spread.at[zh, core], local_sem.at[3 + zh])
        pltpu_copy.start()
        remote = pltpu.make_async_remote_copy(
            src_ref=normed.at[2 * zh + 1 - core], dst_ref=spread.at[zh, core],
            send_sem=tok_send.at[zh], recv_sem=tok_recv.at[zh],
            device_id=partner, device_id_type=MESH)
        remote.start()
        exchange.append((pltpu_copy, remote))
    for mine, remote in exchange:
        mine.wait()
        remote.wait()

    x, y, zown = at["x"], at["y"], at["z"] // 2
    zfar, far_x, far_y = 1 - zown, (x + 2) % 4, (y + 2) % 4

    def weight(c, z, yy, xx):
        index = {"x": xx, "y": yy, "z": z}
        d1, d2, d3 = ORDERS[c]
        return weights[c][index[d3], index[d2], index[d1]]

    def units(yy, xx, parts, first):
        h = 4 * yy + xx
        total = None
        for c, zh in parts:
            rhs = jnp.concatenate(
                [weight(c, 2 * zh, yy, xx), weight(c, 2 * zh + 1, yy, xx)], axis=1)
            term = jnp.dot(spread[zh, :, c].reshape(2 * rows, third), rhs,
                           preferred_element_type=F32)
            total = term if total is None else total + term
        total = total.reshape(2, rows, 256)
        if first:
            acc[h] = total
        else:
            acc[h] += total

    def part(h):
        return pltpu.make_async_remote_copy(
            src_ref=acc.at[h, 1 - core], dst_ref=other.at[h],
            send_sem=part_send.at[h], recv_sem=part_recv.at[h],
            device_id=partner, device_id_type=MESH)

    both = lambda c: [(c, 0), (c, 1)]

    def loop(n, body):
        def step(i, _):
            body(i)
            return 0
        lax.fori_loop(0, n, step, 0)

    def near(at_dim, k):
        return (at_dim + k + k // 2) % 4

    def late(yy, xx, parts):
        units(yy, xx, parts, False)
        part(4 * yy + xx).start()

    receive(2, 0, 1, 3, 2)
    send(2, STEP)
    loop(9, lambda i: units(near(y, i // 3), near(x, i % 3), [(0, zown)] + both(1) + both(2), True))
    loop(3, lambda i: units(near(y, i), far_x, [(0, zown)] + both(2), True))
    loop(3, lambda i: units(far_y, near(x, i), [(0, zown)] + both(1), True))
    units(far_y, far_x, [(0, zown)], True)
    receive(2, STEP)

    def late_group(g):
        @pl.when(g != far_x)
        def _():
            loop(3, lambda i: late(near(y, i), g, [(0, zfar)]))
            late(far_y, g, [(0, zfar)] + both(2))

        @pl.when(g == far_x)
        def _():
            loop(3, lambda i: late(near(y, i), g, [(0, zfar)] + both(1)))
            late(far_y, g, [(0, zfar)] + both(1) + both(2))

    def turned(values, gain):
        mean = jnp.mean(values * values, axis=-1, keepdims=True)
        values = values * lax.rsqrt(mean + 1e-6) * gain
        return values * cos_ref[...] + pltpu.roll(values, 64, 1) * sin_ref[...]

    def in_two(ref, values):
        high = values.astype(BF16)
        ref[:, 0:128] = high
        ref[:, 128:256] = (values - high.astype(F32)).astype(BF16)

    low = lax.broadcasted_iota(jnp.int32, (rows, 128), 1) < 64

    def summed(h, is_query):
        first = acc[h, core, :, 0:128] + other[h, :, 0:128]
        second = acc[h, core, :, 128:256] + other[h, :, 128:256]
        if is_query:
            return jnp.where(low, first, pltpu.roll(second, 64, 1))
        return jnp.where(low, pltpu.roll(first, 64, 1), second)

    def remote(src, dst, send_sem, recv_sem, to):
        return pltpu.make_async_remote_copy(
            src_ref=src, dst_ref=dst, send_sem=send_sem, recv_sem=recv_sem,
            device_id=to, device_id_type=MESH)

    def over_pair(g):
        return remote(kv_out.at[g], kv.at[g, 4 + zlo], pair_send.at[0, g], pair_recv.at[0, g], pair)

    def query_pair(g):
        mine = pl.ds(8 * (1 - zlo) + 2 * g, 2)
        return remote(q_own.at[mine], q_in.at[pl.ds(2 * g, 2)],
                      pair_send.at[1, g], pair_recv.at[1, g], pair)

    def next_run(g, block):
        return remote(kv.at[g, 4 + block], kv.at[g, 2 + block],
                      x_send.at[block, g], x_recv.at[2 + block, g], ahead)

    def second_run(g):
        return remote(kv.at[g, 2], kv.at[g, 0], x_send.at[2, g], x_recv.at[0, g], ahead)

    def to_relay(g, half=1):
        slot = g + 1 - half
        return remote(kv.at[g, 4 + half], relay.at[slot], x_send.at[3, slot],
                      relay_recv.at[slot], relay_by)

    def from_relay(g, half=1):
        slot = g + 1 - half
        return remote(relay.at[slot], kv.at[g, half], x_send.at[4, slot],
                      x_recv.at[half, g], relay_to)

    def when(condition, action):
        @pl.when(condition)
        def _():
            action()

    has_next, has_second = run + 1 < runs, run + 2 < runs
    relays = source_y >= 0

    def send_own(g):
        when(has_next, next_run(g, zlo).start)
        when(has_second & (zlo == 1), to_relay(g).start)
        if isinstance(g, int) and g == LAST:
            when(has_second & (zlo == 0), to_relay(g, 0).start)

    def hop(g):
        over_pair(g).wait_recv()
        when(has_next, next_run(g, 1 - zlo).start)
        when(has_second & (zlo == 0), to_relay(g).start)
        if g == LAST:
            when(has_second & (zlo == 1), to_relay(g, 0).start)

    def forward(g):
        if g == LAST:
            when(relays, to_relay(g, 0).wait_recv)
            when(relays, from_relay(g, 0).start)
        else:
            when(run >= 1, next_run(g, 0).wait_recv)
            when((run >= 1) & has_next, second_run(g).start)
        when(relays, to_relay(g).wait_recv)
        when(relays, from_relay(g).start)

    def key_values(g):
        for mine in (True, False):
            k = 4 * (zlo if mine else 1 - zlo) + g
            keep = kv.at[g, 4 + zlo] if mine else kv_out.at[g]
            part(k).wait_recv()
            part(8 + k).wait_recv()
            in_two(keep, turned(summed(k, False), kg_ref[...]))
            keep[:, 256:384] = summed(8 + k, False).astype(BF16)
        over_pair(g).start()
        when(g < 2, lambda: send_own(g))

    def stage(n):
        when(n < 4, lambda: late_group(n))
        when(n > 0, lambda: key_values(n - 1))

    loop(5, stage)

    query_gain = qg_ref[...] * (QSCALE ** -0.5 * math.log2(math.e))

    def queries(g, mine):
        head = 8 * (zlo if mine else 1 - zlo) + 2 * g
        for i in (0, 1):
            in_two(q_own.at[head + i], turned(summed(head + i, True), query_gain))

    def queries_out(g):
        queries(g, False)
        query_pair(g).start()

    hop(0)
    hop(1)
    loop(4, queries_out)
    forward(0)
    send_own(2)
    hop(2)
    hop(3)
    loop(4, lambda g: queries(g, True))
    loop(16, lambda h: part(h).wait_send())

    row = lax.broadcasted_iota(jnp.int32, (rows, rows), 0)
    col = lax.broadcasted_iota(jnp.int32, (rows, rows), 1)
    causal = col <= row

    def score_steps(slot, g, token_block, q):
        q = q.reshape(2 * rows, 256)
        q_hi, q_lo = q[:, 0:128], q[:, 128:256]
        q = jnp.concatenate([q_hi, q_hi, q_lo, q_lo], axis=1)
        pen = [jnp.where(2 * run - 4 + token_block + m >= 0, 0.0, NEG).astype(F32)
               for m in range(4)]
        best = []

        def score(m):
            keys = kv[g, token_block + m, :, 0:256]
            keys = jnp.concatenate([keys, keys], axis=1)
            out = lax.dot_general(q, keys, (((1,), (1,)), ((), ())), preferred_element_type=F32)
            return out.reshape(2, rows, 256)

        def tile(m):
            if m == 0:
                out = jnp.where(causal[None], score(4), score(0) + pen[0])
            else:
                out = score(m) + pen[m]
            acc[4 * slot + m] = out
            high = jnp.maximum(out[:, :, 0:128], out[:, :, 128:256])
            best.append(jnp.maximum(best[-1], high) if best else high)
            if m == 3:
                top[slot] = jnp.broadcast_to(
                    jnp.max(best[-1], axis=-1, keepdims=True), (2, rows, 128))

        return [functools.partial(tile, m) for m in range(4)]

    def value_steps(slot, g, token_block, keep):
        def one(i):
            high = top[slot, i, :, 0:1]
            w = [jnp.exp2(acc[4 * slot + m, i] - high) for m in range(4)]
            total = jnp.sum((w[0] + w[1]) + (w[2] + w[3]), axis=-1, keepdims=True)
            probs = [jnp.where(causal, 0.0, w[0]), w[1], w[2], w[3], jnp.where(causal, w[0], 0.0)]
            probs = jnp.concatenate([p.astype(BF16) for p in probs], axis=1)
            values = kv[g, pl.ds(token_block, 5), :, 256:384].reshape(5 * rows, 128)
            out = jnp.dot(probs, values, preferred_element_type=F32)
            keep[:, 128 * i:128 * i + 128] = (out * (1.0 / total)).astype(BF16)

        return [functools.partial(one, i) for i in (0, 1)]

    def columns(g):
        return out_ref.at[:, pl.ds(pl.multiple_of((8 * zlo + 2 * g) * 128, 256), 256)]

    def give(g):
        return remote(result.at[1, g], columns(g), out_send.at[g], out_recv.at[g], pair)

    def keep_own(g):
        return pltpu.make_async_copy(result.at[0, g], columns(g), local_sem.at[5 + g])

    def window(g):
        if g == LAST:
            when(run >= 1, next_run(g, 0).wait_recv)
        when(run >= 1, next_run(g, 1).wait_recv)
        when(run >= 2, from_relay(g, 0).wait_recv if g == LAST else second_run(g).wait_recv)
        when(run >= 2, from_relay(g).wait_recv)

    def score_mine(g):
        return score_steps(0, g, zlo, q_own[pl.ds(8 * zlo + 2 * g, 2)])

    def score_theirs(g):
        return score_steps(1, g, 1 - zlo, q_in[pl.ds(2 * g, 2)])

    def value_mine(g):
        return value_steps(0, g, zlo, result.at[0, g])

    def value_theirs(g):
        return value_steps(1, g, 1 - zlo, result.at[1, g])

    def together(scores, values):
        for n in (0, 4, 1, 2, 5, 3):
            steps = values if n >= 4 else scores
            if steps:
                steps[n % 4]()

    forward(1)
    send_own(3)
    window(0)
    together(score_mine(0), [])
    for g in range(4):
        query_pair(g).wait_recv()
        together(score_theirs(g), value_mine(g))
        keep_own(g).start()
        if g == 0:
            forward(2)
            forward(3)
        if g < 3:
            window(g + 1)
        together(score_mine(g + 1) if g < 3 else [], value_theirs(g))
        give(g).start()

    for copy in sent:
        copy.wait_send()

    for g in range(4):
        over_pair(g).wait_send()
        query_pair(g).wait_send()
        when(has_next, next_run(g, 0).wait_send)
        when(has_next, next_run(g, 1).wait_send)
        if g == LAST:
            when(has_second, to_relay(g, 0).wait_send)
            when(relays, from_relay(g, 0).wait_send)
        else:
            when((run >= 1) & has_next, second_run(g).wait_send)
        when(has_second, to_relay(g).wait_send)
        when(relays, from_relay(g).wait_send)
        keep_own(g).wait()
        give(g).wait()


def on_device(tokens, norm_gain, w_query, w_keyval, q_gain, k_gain):
    rows, width = tokens.shape[1:]
    quarter, cols = w_query.shape
    heads = cols * lax.axis_size("seq") // q_gain.shape[0]
    half = q_gain.shape[0] // 2
    third = quarter // 3
    shard = jnp.concatenate([w_query, w_keyval], axis=1).reshape(3, third, 2 * cols)
    place = (lax.axis_index("seq") * rows + jnp.arange(rows)).astype(F32)
    freq = jnp.power(10000.0, -2.0 * (jnp.arange(2 * half) % half).astype(F32) / (2 * half))
    angle = place[:, None] * freq[None, :]
    cos = jnp.cos(angle)
    sin = jnp.where(jnp.arange(2 * half) < half, -1.0, 1.0) * jnp.sin(angle)
    vmem = pl.BlockSpec(memory_space=pltpu.VMEM)
    anyspace = pl.BlockSpec(memory_space=pl.ANY)
    dma = pltpu.SemaphoreType.DMA
    block = pltpu.VMEM((4, 4, 4, third, 128), BF16)
    out = pl.pallas_call(
        layer_kernel,
        name="layer",
        out_shape=jax.ShapeDtypeStruct((rows, heads * 128), BF16),
        in_specs=[anyspace, vmem, anyspace, anyspace, anyspace, vmem, vmem],
        out_specs=vmem,
        scratch_shapes=[
            block, block, block,
            pltpu.VMEM((rows, width), BF16),
            pltpu.VMEM((rows, 128), F32),
            pltpu.VMEM((rows, 128), F32),
            pltpu.VMEM((4, 3, rows, third), BF16),
            pltpu.VMEM((2, 2, 3, rows, third), BF16),
            pltpu.VMEM((heads, 2, rows, 256), F32),
            pltpu.VMEM((2, 2, rows, 128), F32),
            pltpu.VMEM((heads, rows, 256), F32),
            pltpu.VMEM((heads, rows, 256), BF16),
            pltpu.VMEM((heads // 2, rows, 256), BF16),
            pltpu.VMEM((4, rows, 384), BF16),
            pltpu.VMEM((4, 6, rows, 384), BF16),
            pltpu.VMEM((5, rows, 384), BF16),
            pltpu.VMEM((2, 4, rows, 256), BF16),
            dma((12,)), dma((3, 3, 5, 2)), dma((3, 3, 5, 2)),
            dma((2,)), dma((2,)), dma((heads,)), dma((heads,)),
            dma((2, 4)), dma((2, 4)), dma((5, 5)), dma((4, 4)), dma((5,)),
            dma((4,)), dma((4,)),
        ],
        compiler_params=pltpu.CompilerParams(
            collective_id=0, has_side_effects=True, vmem_limit_bytes=62 * 2**20),
    )(tokens[0], norm_gain.reshape(-1, 128), shard, cos, sin,
      q_gain[None], k_gain[None])
    return out[None]


def solution(mesh):
    in_specs = (P("fsdp", "seq", None), P(), P("fsdp", "seq"), P("fsdp", "seq"), P(), P())
    out_specs = P("fsdp", "seq", None)
    return jax.shard_map(
        on_device, mesh=mesh, in_specs=in_specs, out_specs=out_specs, check_vma=False
    )
```

```python
import functools
import math

import jax
import jax.numpy as jnp
from jax import lax
from jax.experimental import pallas as pl
from jax.experimental.pallas import tpu as pltpu
from jax.sharding import PartitionSpec as P

WINDOW = 1024
QSCALE = 168
MESH = pl.DeviceIdType.MESH
F32 = jnp.float32
BF16 = jnp.bfloat16
NEG = -1e30
LAST = 3
STEP = 4

ORDERS = (("x", "y", "z"), ("y", "z", "x"), ("z", "x", "y"))


def position():
    f, s = lax.axis_index("fsdp"), lax.axis_index("seq")
    return {"x": (s // 2) % 4, "y": s // 8, "z": 2 * (f // 2) + s % 2}, f % 2


def device(at, core):
    return (2 * (at["z"] // 2) + core, 8 * at["y"] + 2 * at["x"] + at["z"] % 2)


def shifted(at, dim, by):
    moved = dict(at)
    moved[dim] = (at[dim] + by + 4) % 4
    return moved


def layer_kernel(
    tok_hbm, gain_ref, wq_ref, wkv_ref, cos_hbm, sin_hbm, qg_ref, kg_ref,
    out_ref,
    w0, w1, w2, tok, cos_ref, sin_ref,
    normed, spread, acc, top, other, q_own, q_in, kv_out, kv, relay, result,
    local_sem, ring_send, ring_recv, tok_send, tok_recv, part_send, part_recv,
    pair_send, pair_recv, x_send, x_recv, relay_recv, out_send, out_recv,
):
    at, core = position()
    partner = device(at, 1 - core)
    rows, third = tok.shape[0], w0.shape[3]
    weights = (w0, w1, w2)
    f, s = lax.axis_index("fsdp"), lax.axis_index("seq")
    zlo = s % 2
    run = s // 2
    runs = 16

    def on_row(xx, yy):
        return device({"x": (xx + 4) % 4, "y": (yy + 4) % 4, "z": at["z"]}, core)

    relay_by = on_row(at["x"] - 1, at["y"] + at["x"] // 2)
    source_x = (at["x"] + 1) % 4
    source_y = at["y"] - source_x // 2
    relay_from = on_row(source_x, source_y)
    relay_to = on_row(at["x"] - 1, at["y"])
    ahead = (f, (s + 2) % (2 * runs))
    behind = (f, (s - 2 + 2 * runs) % (2 * runs))
    pair = (f, s + 1 - 2 * zlo)

    barrier = pltpu.get_barrier_semaphore()
    peers = [device(shifted(at, d, by), core) for d in "xyz" for by in (1, -1)]
    peers += [partner, ahead, behind, relay_by, relay_from]
    for peer in peers:
        pl.semaphore_signal(barrier, inc=1, device_id=peer, device_id_type=MESH)

    def clear(first, absent):
        @pl.when(absent)
        def _():
            kv[:, first:first + 2] = jnp.zeros((4, 2) + kv.shape[2:], BF16)

    clear(0, run < 2)
    clear(2, run < 1)

    fetched = [
        pltpu.make_async_copy(tok_hbm, tok, local_sem.at[9]),
        pltpu.make_async_copy(cos_hbm, cos_ref, local_sem.at[10]),
        pltpu.make_async_copy(sin_hbm, sin_ref, local_sem.at[11]),
    ]
    for copy in fetched:
        copy.start()
    packed = jnp.concatenate([wq_ref[...], wkv_ref[...]], axis=0).astype(F32)
    packed = jnp.concatenate([packed, jnp.zeros((128, 64), F32)], axis=1).T.astype(BF16)
    for c, (d1, d2, d3) in enumerate(ORDERS):
        weights[c][at[d3], at[d2], at[d1]] = packed[c * third:(c + 1) * third]
    pl.semaphore_wait(barrier, len(peers))

    sent = []

    def block(c, phase, index, part, half):
        d1, d2, d3 = ORDERS[c]
        w = weights[c]
        if phase == 0:
            if half is None:
                return w.at[at[d3], at[d2], index]
            return w.at[at[d3], at[d2], index, pl.ds(half * (third // 2), third // 2)]
        bundle = w.at[at[d3], index] if phase == 1 else w.at[index]
        if half is None:
            return bundle.at[(at[(d1, d2)[phase - 1]] + part) % 4]
        return bundle.at[pl.ds(2 * half, 2)]

    flying = {}

    def send(phase, *parts):
        for c in range(3):
            dim = ORDERS[c][phase]
            for part in parts:
                copies = []
                for side, by in enumerate((1, -1)):
                    if part == STEP:
                        ref = block(c, phase, shifted(at, dim, -by)[dim], None, side)
                    else:
                        ref = block(c, phase, at[dim], part, None)
                    copies.append(pltpu.make_async_remote_copy(
                        src_ref=ref, dst_ref=ref,
                        send_sem=ring_send.at[c, phase, part, side],
                        recv_sem=ring_recv.at[c, phase, part, side],
                        device_id=device(shifted(at, dim, by), core), device_id_type=MESH))
                    copies[-1].start()
                sent.extend(copies)
                flying[c, phase, part] = copies

    def receive(phase, *parts):
        for c in range(3):
            for part in parts:
                for copy in flying[c, phase, part]:
                    copy.wait_recv()

    send(0, 0)
    receive(0, 0)
    for phase in (0, 1):
        send(phase, STEP)
        send(phase + 1, 0, 1, 3)
        receive(phase, STEP)
        send(phase + 1, 2)
        if phase == 0:
            receive(1, 0, 1, 3, 2)

    strip = 32
    for copy in fetched:
        copy.wait()
    gain = jnp.concatenate([gain_ref[j:j + 1] for j in range(gain_ref.shape[0])], axis=1)

    def norm_rows(i, _):
        at_row = pl.ds(pl.multiple_of(i * strip, strip), strip)
        flat = tok[at_row, :].astype(F32)
        mean = jnp.mean(flat * flat, axis=-1, keepdims=True)
        out = (flat * lax.rsqrt(mean + 1e-6) * gain).astype(BF16)
        for k in range(4):
            for c in range(3):
                j = 3 * k + c
                normed[k, c, at_row, :] = out[:, j * third:(j + 1) * third]
        return 0

    lax.fori_loop(0, rows // strip, norm_rows, 0)
    exchange = []
    for zh in range(2):
        pltpu_copy = pltpu.make_async_copy(
            normed.at[2 * zh + core], spread.at[zh, core], local_sem.at[3 + zh])
        pltpu_copy.start()
        remote = pltpu.make_async_remote_copy(
            src_ref=normed.at[2 * zh + 1 - core], dst_ref=spread.at[zh, core],
            send_sem=tok_send.at[zh], recv_sem=tok_recv.at[zh],
            device_id=partner, device_id_type=MESH)
        remote.start()
        exchange.append((pltpu_copy, remote))
    for mine, remote in exchange:
        mine.wait()
        remote.wait()

    x, y, zown = at["x"], at["y"], at["z"] // 2
    zfar, far_x, far_y = 1 - zown, (x + 2) % 4, (y + 2) % 4

    def weight(c, z, yy, xx):
        index = {"x": xx, "y": yy, "z": z}
        d1, d2, d3 = ORDERS[c]
        return weights[c][index[d3], index[d2], index[d1]]

    def units(yy, xx, parts, first):
        h = 4 * yy + xx
        total = None
        for c, zh in parts:
            rhs = jnp.concatenate(
                [weight(c, 2 * zh, yy, xx), weight(c, 2 * zh + 1, yy, xx)], axis=1)
            term = jnp.dot(spread[zh, :, c].reshape(2 * rows, third), rhs,
                           preferred_element_type=F32)
            total = term if total is None else total + term
        total = total.reshape(2, rows, 256)
        if first:
            acc[h] = total
        else:
            acc[h] += total

    def part(h):
        return pltpu.make_async_remote_copy(
            src_ref=acc.at[h, 1 - core], dst_ref=other.at[h],
            send_sem=part_send.at[h], recv_sem=part_recv.at[h],
            device_id=partner, device_id_type=MESH)

    both = lambda c: [(c, 0), (c, 1)]

    def loop(n, body):
        def step(i, _):
            body(i)
            return 0
        lax.fori_loop(0, n, step, 0)

    def near(at_dim, k):
        return (at_dim + k + k // 2) % 4

    def late(yy, xx, parts):
        units(yy, xx, parts, False)
        part(4 * yy + xx).start()

    receive(2, 0, 1, 3, 2)
    send(2, STEP)
    loop(9, lambda i: units(near(y, i // 3), near(x, i % 3), [(0, zown)] + both(1) + both(2), True))
    loop(3, lambda i: units(near(y, i), far_x, [(0, zown)] + both(2), True))
    loop(3, lambda i: units(far_y, near(x, i), [(0, zown)] + both(1), True))
    units(far_y, far_x, [(0, zown)], True)
    receive(2, STEP)

    def late_group(g):
        @pl.when(g != far_x)
        def _():
            loop(3, lambda i: late(near(y, i), g, [(0, zfar)]))
            late(far_y, g, [(0, zfar)] + both(2))

        @pl.when(g == far_x)
        def _():
            loop(3, lambda i: late(near(y, i), g, [(0, zfar)] + both(1)))
            late(far_y, g, [(0, zfar)] + both(1) + both(2))

    def turned(values, gain):
        mean = jnp.mean(values * values, axis=-1, keepdims=True)
        values = values * lax.rsqrt(mean + 1e-6) * gain
        return values * cos_ref[...] + pltpu.roll(values, 64, 1) * sin_ref[...]

    def in_two(ref, values):
        high = values.astype(BF16)
        ref[:, 0:128] = high
        ref[:, 128:256] = (values - high.astype(F32)).astype(BF16)

    low = lax.broadcasted_iota(jnp.int32, (rows, 128), 1) < 64

    def summed(h, is_query):
        first = acc[h, core, :, 0:128] + other[h, :, 0:128]
        second = acc[h, core, :, 128:256] + other[h, :, 128:256]
        if is_query:
            return jnp.where(low, first, pltpu.roll(second, 64, 1))
        return jnp.where(low, pltpu.roll(first, 64, 1), second)

    def remote(src, dst, send_sem, recv_sem, to):
        return pltpu.make_async_remote_copy(
            src_ref=src, dst_ref=dst, send_sem=send_sem, recv_sem=recv_sem,
            device_id=to, device_id_type=MESH)

    def over_pair(g):
        return remote(kv_out.at[g], kv.at[g, 4 + zlo], pair_send.at[0, g], pair_recv.at[0, g], pair)

    def query_pair(g):
        mine = pl.ds(8 * (1 - zlo) + 2 * g, 2)
        return remote(q_own.at[mine], q_in.at[pl.ds(2 * g, 2)],
                      pair_send.at[1, g], pair_recv.at[1, g], pair)

    def next_run(g, block):
        return remote(kv.at[g, 4 + block], kv.at[g, 2 + block],
                      x_send.at[block, g], x_recv.at[2 + block, g], ahead)

    def second_run(g):
        return remote(kv.at[g, 2], kv.at[g, 0], x_send.at[2, g], x_recv.at[0, g], ahead)

    def to_relay(g, half=1):
        slot = g + 1 - half
        return remote(kv.at[g, 4 + half], relay.at[slot], x_send.at[3, slot],
                      relay_recv.at[slot], relay_by)

    def from_relay(g, half=1):
        slot = g + 1 - half
        return remote(relay.at[slot], kv.at[g, half], x_send.at[4, slot],
                      x_recv.at[half, g], relay_to)

    def when(condition, action):
        @pl.when(condition)
        def _():
            action()

    has_next, has_second = run + 1 < runs, run + 2 < runs
    relays = source_y >= 0

    def send_own(g):
        when(has_next, next_run(g, zlo).start)
        when(has_second & (zlo == 1), to_relay(g).start)
        if isinstance(g, int) and g == LAST:
            when(has_second & (zlo == 0), to_relay(g, 0).start)

    def hop(g):
        over_pair(g).wait_recv()
        when(has_next, next_run(g, 1 - zlo).start)
        when(has_second & (zlo == 0), to_relay(g).start)
        if g == LAST:
            when(has_second & (zlo == 1), to_relay(g, 0).start)

    def forward(g):
        if g == LAST:
            when(relays, to_relay(g, 0).wait_recv)
            when(relays, from_relay(g, 0).start)
        else:
            when(run >= 1, next_run(g, 0).wait_recv)
            when((run >= 1) & has_next, second_run(g).start)
        when(relays, to_relay(g).wait_recv)
        when(relays, from_relay(g).start)

    def key_values(g):
        for mine in (True, False):
            k = 4 * (zlo if mine else 1 - zlo) + g
            keep = kv.at[g, 4 + zlo] if mine else kv_out.at[g]
            part(k).wait_recv()
            part(8 + k).wait_recv()
            in_two(keep, turned(summed(k, False), kg_ref[...]))
            keep[:, 256:384] = summed(8 + k, False).astype(BF16)
        over_pair(g).start()
        when(g < 2, lambda: send_own(g))

    def stage(n):
        when(n < 4, lambda: late_group(n))
        when(n > 0, lambda: key_values(n - 1))

    loop(5, stage)

    query_gain = qg_ref[...] * (QSCALE ** -0.5 * math.log2(math.e))

    def queries(g, mine):
        head = 8 * (zlo if mine else 1 - zlo) + 2 * g
        for i in (0, 1):
            in_two(q_own.at[head + i], turned(summed(head + i, True), query_gain))

    def queries_out(g):
        queries(g, False)
        query_pair(g).start()

    hop(0)
    hop(1)
    loop(4, queries_out)
    forward(0)
    send_own(2)
    hop(2)
    hop(3)
    loop(4, lambda g: queries(g, True))
    loop(16, lambda h: part(h).wait_send())

    row = lax.broadcasted_iota(jnp.int32, (rows, rows), 0)
    col = lax.broadcasted_iota(jnp.int32, (rows, rows), 1)
    causal = col <= row

    def score_steps(slot, g, token_block, q):
        q = q.reshape(2 * rows, 256)
        q_hi, q_lo = q[:, 0:128], q[:, 128:256]
        q = jnp.concatenate([q_hi, q_hi, q_lo, q_lo], axis=1)
        pen = [jnp.where(2 * run - 4 + token_block + m >= 0, 0.0, NEG).astype(F32)
               for m in range(4)]
        best = []

        def score(m):
            keys = kv[g, token_block + m, :, 0:256]
            keys = jnp.concatenate([keys, keys], axis=1)
            out = lax.dot_general(q, keys, (((1,), (1,)), ((), ())), preferred_element_type=F32)
            return out.reshape(2, rows, 256)

        def tile(m):
            if m == 0:
                out = jnp.where(causal[None], score(4), score(0) + pen[0])
            else:
                out = score(m) + pen[m]
            acc[4 * slot + m] = out
            high = jnp.maximum(out[:, :, 0:128], out[:, :, 128:256])
            best.append(jnp.maximum(best[-1], high) if best else high)
            if m == 3:
                top[slot] = jnp.broadcast_to(
                    jnp.max(best[-1], axis=-1, keepdims=True), (2, rows, 128))

        return [functools.partial(tile, m) for m in range(4)]

    def value_steps(slot, g, token_block, keep):
        def one(i):
            high = top[slot, i, :, 0:1]
            w = [jnp.exp2(acc[4 * slot + m, i] - high) for m in range(4)]
            total = jnp.sum((w[0] + w[1]) + (w[2] + w[3]), axis=-1, keepdims=True)
            inv = 1.0 / total
            w = [v * inv for v in w]
            probs = [jnp.where(causal, 0.0, w[0]), w[1], w[2], w[3], jnp.where(causal, w[0], 0.0)]
            probs = jnp.concatenate([p.astype(BF16) for p in probs], axis=1)
            values = kv[g, pl.ds(token_block, 5), :, 256:384].reshape(5 * rows, 128)
            out = jnp.dot(probs, values, preferred_element_type=F32)
            keep[:, 128 * i:128 * i + 128] = out.astype(BF16)

        return [functools.partial(one, i) for i in (0, 1)]

    def columns(g):
        return out_ref.at[:, pl.ds(pl.multiple_of((8 * zlo + 2 * g) * 128, 256), 256)]

    def give(g):
        return remote(result.at[1, g], columns(g), out_send.at[g], out_recv.at[g], pair)

    def keep_own(g):
        return pltpu.make_async_copy(result.at[0, g], columns(g), local_sem.at[5 + g])

    def window(g):
        if g == LAST:
            when(run >= 1, next_run(g, 0).wait_recv)
        when(run >= 1, next_run(g, 1).wait_recv)
        when(run >= 2, from_relay(g, 0).wait_recv if g == LAST else second_run(g).wait_recv)
        when(run >= 2, from_relay(g).wait_recv)

    def score_mine(g):
        return score_steps(0, g, zlo, q_own[pl.ds(8 * zlo + 2 * g, 2)])

    def score_theirs(g):
        return score_steps(1, g, 1 - zlo, q_in[pl.ds(2 * g, 2)])

    def value_mine(g):
        return value_steps(0, g, zlo, result.at[0, g])

    def value_theirs(g):
        return value_steps(1, g, 1 - zlo, result.at[1, g])

    def together(scores, values):
        for n in (0, 4, 1, 2, 5, 3):
            steps = values if n >= 4 else scores
            if steps:
                steps[n % 4]()

    forward(1)
    send_own(3)
    window(0)
    together(score_mine(0), [])
    for g in range(4):
        query_pair(g).wait_recv()
        together(score_theirs(g), value_mine(g))
        keep_own(g).start()
        if g == 0:
            forward(2)
            forward(3)
        if g < 3:
            window(g + 1)
        together(score_mine(g + 1) if g < 3 else [], value_theirs(g))
        give(g).start()

    for copy in sent:
        copy.wait_send()

    for g in range(4):
        over_pair(g).wait_send()
        query_pair(g).wait_send()
        when(has_next, next_run(g, 0).wait_send)
        when(has_next, next_run(g, 1).wait_send)
        if g == LAST:
            when(has_second, to_relay(g, 0).wait_send)
            when(relays, from_relay(g, 0).wait_send)
        else:
            when((run >= 1) & has_next, second_run(g).wait_send)
        when(has_second, to_relay(g).wait_send)
        when(relays, from_relay(g).wait_send)
        keep_own(g).wait()
        give(g).wait()


def on_device(tokens, norm_gain, w_query, w_keyval, q_gain, k_gain):
    rows, width = tokens.shape[1:]
    quarter, cols = w_query.shape
    heads = cols * lax.axis_size("seq") // q_gain.shape[0]
    half = q_gain.shape[0] // 2
    third = quarter // 3
    place = (lax.axis_index("seq") * rows + jnp.arange(rows)).astype(F32)
    freq = jnp.power(10000.0, -2.0 * (jnp.arange(2 * half) % half).astype(F32) / (2 * half))
    angle = place[:, None] * freq[None, :]
    cos = jnp.cos(angle)
    sin = jnp.where(jnp.arange(2 * half) < half, -1.0, 1.0) * jnp.sin(angle)
    vmem = pl.BlockSpec(memory_space=pltpu.VMEM)
    anyspace = pl.BlockSpec(memory_space=pl.ANY)
    dma = pltpu.SemaphoreType.DMA
    block = pltpu.VMEM((4, 4, 4, third, 128), BF16)
    out = pl.pallas_call(
        layer_kernel,
        name="layer",
        out_shape=jax.ShapeDtypeStruct((rows, heads * 128), BF16),
        in_specs=[anyspace, vmem, vmem, vmem, anyspace, anyspace, vmem, vmem],
        out_specs=vmem,
        scratch_shapes=[
            block, block, block,
            pltpu.VMEM((rows, width), BF16),
            pltpu.VMEM((rows, 128), F32),
            pltpu.VMEM((rows, 128), F32),
            pltpu.VMEM((4, 3, rows, third), BF16),
            pltpu.VMEM((2, 2, 3, rows, third), BF16),
            pltpu.VMEM((heads, 2, rows, 256), F32),
            pltpu.VMEM((2, 2, rows, 128), F32),
            pltpu.VMEM((heads, rows, 256), F32),
            pltpu.VMEM((heads, rows, 256), BF16),
            pltpu.VMEM((heads // 2, rows, 256), BF16),
            pltpu.VMEM((4, rows, 384), BF16),
            pltpu.VMEM((4, 6, rows, 384), BF16),
            pltpu.VMEM((5, rows, 384), BF16),
            pltpu.VMEM((2, 4, rows, 256), BF16),
            dma((12,)), dma((3, 3, 5, 2)), dma((3, 3, 5, 2)),
            dma((2,)), dma((2,)), dma((heads,)), dma((heads,)),
            dma((2, 4)), dma((2, 4)), dma((5, 5)), dma((4, 4)), dma((5,)),
            dma((4,)), dma((4,)),
        ],
        compiler_params=pltpu.CompilerParams(
            collective_id=0, has_side_effects=True, vmem_limit_bytes=62 * 2**20),
    )(tokens[0], norm_gain.reshape(-1, 128), w_query.T, w_keyval.T, cos, sin,
      q_gain[None], k_gain[None])
    return out[None]


def solution(mesh):
    in_specs = (P("fsdp", "seq", None), P(), P("fsdp", "seq"), P("fsdp", "seq"), P(), P())
    out_specs = P("fsdp", "seq", None)
    return jax.shard_map(
        on_device, mesh=mesh, in_specs=in_specs, out_specs=out_specs, check_vma=False
    )
```

```python
import functools
import math

import jax
import jax.numpy as jnp
from jax import lax
from jax.experimental import pallas as pl
from jax.experimental.pallas import tpu as pltpu
from jax.sharding import PartitionSpec as P

WINDOW = 1024
QSCALE = 168
MESH = pl.DeviceIdType.MESH
F32 = jnp.float32
BF16 = jnp.bfloat16
NEG = -1e30
LAST = 3
STEP = 4

ORDERS = (("x", "y", "z"), ("y", "z", "x"), ("z", "x", "y"))


def position():
    f, s = lax.axis_index("fsdp"), lax.axis_index("seq")
    return {"x": (s // 2) % 4, "y": s // 8, "z": 2 * (f // 2) + s % 2}, f % 2


def device(at, core):
    return (2 * (at["z"] // 2) + core, 8 * at["y"] + 2 * at["x"] + at["z"] % 2)


def shifted(at, dim, by):
    moved = dict(at)
    moved[dim] = (at[dim] + by + 4) % 4
    return moved


def layer_kernel(
    tok_hbm, gain_ref, wq_ref, wkv_ref, cos_hbm, sin_hbm, qg_ref, kg_ref,
    out_ref,
    w0, w1, w2, tok, cos_ref, sin_ref,
    normed, spread, acc, top, other, q_own, q_in, kv_out, kv, relay, result,
    local_sem, ring_send, ring_recv, tok_send, tok_recv, part_send, part_recv,
    pair_send, pair_recv, x_send, x_recv, relay_recv, out_send, out_recv,
):
    at, core = position()
    partner = device(at, 1 - core)
    rows, third = tok.shape[0], w0.shape[3]
    weights = (w0, w1, w2)
    f, s = lax.axis_index("fsdp"), lax.axis_index("seq")
    zlo = s % 2
    run = s // 2
    runs = 16

    def on_row(xx, yy):
        return device({"x": (xx + 4) % 4, "y": (yy + 4) % 4, "z": at["z"]}, core)

    relay_by = on_row(at["x"] - 1, at["y"] + at["x"] // 2)
    source_x = (at["x"] + 1) % 4
    source_y = at["y"] - source_x // 2
    relay_from = on_row(source_x, source_y)
    relay_to = on_row(at["x"] - 1, at["y"])
    ahead = (f, (s + 2) % (2 * runs))
    behind = (f, (s - 2 + 2 * runs) % (2 * runs))
    pair = (f, s + 1 - 2 * zlo)

    barrier = pltpu.get_barrier_semaphore()
    peers = [device(shifted(at, d, by), core) for d in "xyz" for by in (1, -1)]
    peers += [partner, ahead, behind, relay_by, relay_from]
    for peer in peers:
        pl.semaphore_signal(barrier, inc=1, device_id=peer, device_id_type=MESH)

    def clear(first, absent):
        @pl.when(absent)
        def _():
            kv[:, first:first + 2] = jnp.zeros((4, 2) + kv.shape[2:], BF16)

    clear(0, run < 2)
    clear(2, run < 1)

    fetched = [
        pltpu.make_async_copy(tok_hbm, tok, local_sem.at[9]),
        pltpu.make_async_copy(cos_hbm, cos_ref, local_sem.at[10]),
        pltpu.make_async_copy(sin_hbm, sin_ref, local_sem.at[11]),
    ]
    for copy in fetched:
        copy.start()
    packed = jnp.concatenate([wq_ref[...], wkv_ref[...]], axis=0).astype(F32)
    packed = jnp.concatenate([packed, jnp.zeros((128, 64), F32)], axis=1).T.astype(BF16)
    for c, (d1, d2, d3) in enumerate(ORDERS):
        weights[c][at[d3], at[d2], at[d1]] = packed[c * third:(c + 1) * third]
    pl.semaphore_wait(barrier, len(peers))

    sent = []

    def block(c, phase, index, part, half):
        d1, d2, d3 = ORDERS[c]
        w = weights[c]
        if phase == 0:
            if half is None:
                return w.at[at[d3], at[d2], index]
            return w.at[at[d3], at[d2], index, pl.ds(half * (third // 2), third // 2)]
        bundle = w.at[at[d3], index] if phase == 1 else w.at[index]
        if half is None:
            return bundle.at[(at[(d1, d2)[phase - 1]] + part) % 4]
        return bundle.at[pl.ds(2 * half, 2)]

    flying = {}

    def send(phase, *parts):
        for c in range(3):
            dim = ORDERS[c][phase]
            for part in parts:
                copies = []
                for side, by in enumerate((1, -1)):
                    if part == STEP:
                        ref = block(c, phase, shifted(at, dim, -by)[dim], None, side)
                    else:
                        ref = block(c, phase, at[dim], part, None)
                    copies.append(pltpu.make_async_remote_copy(
                        src_ref=ref, dst_ref=ref,
                        send_sem=ring_send.at[c, phase, part, side],
                        recv_sem=ring_recv.at[c, phase, part, side],
                        device_id=device(shifted(at, dim, by), core), device_id_type=MESH))
                    copies[-1].start()
                sent.extend(copies)
                flying[c, phase, part] = copies

    def receive(phase, *parts):
        for c in range(3):
            for part in parts:
                for copy in flying[c, phase, part]:
                    copy.wait_recv()

    send(0, 0)
    receive(0, 0)
    for phase in (0, 1):
        send(phase, STEP)
        send(phase + 1, 0, 1, 3)
        receive(phase, STEP)
        send(phase + 1, 2)
        if phase == 0:
            receive(1, 0, 1, 3, 2)

    strip = 32
    for copy in fetched:
        copy.wait()
    gain = jnp.concatenate([gain_ref[j:j + 1] for j in range(gain_ref.shape[0])], axis=1)

    def norm_rows(i, _):
        at_row = pl.ds(pl.multiple_of(i * strip, strip), strip)
        flat = tok[at_row, :].astype(F32)
        mean = jnp.mean(flat * flat, axis=-1, keepdims=True)
        out = (flat * lax.rsqrt(mean + 1e-6) * gain).astype(BF16)
        for k in range(4):
            for c in range(3):
                j = 3 * k + c
                normed[k, c, at_row, :] = out[:, j * third:(j + 1) * third]
        return 0

    lax.fori_loop(0, rows // strip, norm_rows, 0)
    exchange = []
    for zh in range(2):
        pltpu_copy = pltpu.make_async_copy(
            normed.at[2 * zh + core], spread.at[zh, core], local_sem.at[3 + zh])
        pltpu_copy.start()
        remote = pltpu.make_async_remote_copy(
            src_ref=normed.at[2 * zh + 1 - core], dst_ref=spread.at[zh, core],
            send_sem=tok_send.at[zh], recv_sem=tok_recv.at[zh],
            device_id=partner, device_id_type=MESH)
        remote.start()
        exchange.append((pltpu_copy, remote))
    for mine, remote in exchange:
        mine.wait()
        remote.wait()

    x, y, zown = at["x"], at["y"], at["z"] // 2
    zfar, far_x, far_y = 1 - zown, (x + 2) % 4, (y + 2) % 4

    def weight(c, z, yy, xx):
        index = {"x": xx, "y": yy, "z": z}
        d1, d2, d3 = ORDERS[c]
        return weights[c][index[d3], index[d2], index[d1]]

    def units(yy, xx, parts, first):
        h = 4 * yy + xx
        total = None
        for c, zh in parts:
            rhs = jnp.concatenate(
                [weight(c, 2 * zh, yy, xx), weight(c, 2 * zh + 1, yy, xx)], axis=1)
            term = jnp.dot(spread[zh, :, c].reshape(2 * rows, third), rhs,
                           preferred_element_type=F32)
            total = term if total is None else total + term
        total = total.reshape(2, rows, 256)
        if first:
            acc[h] = total
        else:
            acc[h] += total

    def part(h):
        return pltpu.make_async_remote_copy(
            src_ref=acc.at[h, 1 - core], dst_ref=other.at[h],
            send_sem=part_send.at[h], recv_sem=part_recv.at[h],
            device_id=partner, device_id_type=MESH)

    both = lambda c: [(c, 0), (c, 1)]

    def loop(n, body):
        def step(i, _):
            body(i)
            return 0
        lax.fori_loop(0, n, step, 0)

    def near(at_dim, k):
        return (at_dim + k + k // 2) % 4

    def late(yy, xx, parts):
        units(yy, xx, parts, False)
        part(4 * yy + xx).start()

    receive(2, 0, 1, 3, 2)
    send(2, STEP)
    loop(9, lambda i: units(near(y, i // 3), near(x, i % 3), [(0, zown)] + both(1) + both(2), True))
    loop(3, lambda i: units(near(y, i), far_x, [(0, zown)] + both(2), True))
    loop(3, lambda i: units(far_y, near(x, i), [(0, zown)] + both(1), True))
    units(far_y, far_x, [(0, zown)], True)
    receive(2, STEP)

    def late_group(g):
        @pl.when(g != far_x)
        def _():
            loop(3, lambda i: late(near(y, i), g, [(0, zfar)]))
            late(far_y, g, [(0, zfar)] + both(2))

        @pl.when(g == far_x)
        def _():
            loop(3, lambda i: late(near(y, i), g, [(0, zfar)] + both(1)))
            late(far_y, g, [(0, zfar)] + both(1) + both(2))

    def turned(values, gain):
        mean = jnp.mean(values * values, axis=-1, keepdims=True)
        values = values * lax.rsqrt(mean + 1e-6) * gain
        return values * cos_ref[...] + pltpu.roll(values, 64, 1) * sin_ref[...]

    def in_two(ref, values):
        high = values.astype(BF16)
        ref[:, 0:128] = high
        ref[:, 128:256] = (values - high.astype(F32)).astype(BF16)

    low = lax.broadcasted_iota(jnp.int32, (rows, 128), 1) < 64

    def summed(h, is_query):
        first = acc[h, core, :, 0:128] + other[h, :, 0:128]
        second = acc[h, core, :, 128:256] + other[h, :, 128:256]
        if is_query:
            return jnp.where(low, first, pltpu.roll(second, 64, 1))
        return jnp.where(low, pltpu.roll(first, 64, 1), second)

    def remote(src, dst, send_sem, recv_sem, to):
        return pltpu.make_async_remote_copy(
            src_ref=src, dst_ref=dst, send_sem=send_sem, recv_sem=recv_sem,
            device_id=to, device_id_type=MESH)

    def over_pair(g):
        return remote(kv_out.at[g], kv.at[g, 4 + zlo], pair_send.at[0, g], pair_recv.at[0, g], pair)

    def query_pair(g):
        mine = pl.ds(8 * (1 - zlo) + 2 * g, 2)
        return remote(q_own.at[mine], q_in.at[pl.ds(2 * g, 2)],
                      pair_send.at[1, g], pair_recv.at[1, g], pair)

    def next_run(g, block):
        return remote(kv.at[g, 4 + block], kv.at[g, 2 + block],
                      x_send.at[block, g], x_recv.at[2 + block, g], ahead)

    def second_run(g):
        return remote(kv.at[g, 2], kv.at[g, 0], x_send.at[2, g], x_recv.at[0, g], ahead)

    def to_relay(g, half=1):
        slot = g + 1 - half
        return remote(kv.at[g, 4 + half], relay.at[slot], x_send.at[3, slot],
                      relay_recv.at[slot], relay_by)

    def from_relay(g, half=1):
        slot = g + 1 - half
        return remote(relay.at[slot], kv.at[g, half], x_send.at[4, slot],
                      x_recv.at[half, g], relay_to)

    def when(condition, action):
        @pl.when(condition)
        def _():
            action()

    has_next, has_second = run + 1 < runs, run + 2 < runs
    relays = source_y >= 0

    def send_own(g):
        when(has_next, next_run(g, zlo).start)
        when(has_second & (zlo == 1), to_relay(g).start)
        if isinstance(g, int) and g == LAST:
            when(has_second & (zlo == 0), to_relay(g, 0).start)

    def hop(g):
        over_pair(g).wait_recv()
        when(has_next, next_run(g, 1 - zlo).start)
        when(has_second & (zlo == 0), to_relay(g).start)
        if g == LAST:
            when(has_second & (zlo == 1), to_relay(g, 0).start)

    def forward(g):
        if g == LAST:
            when(relays, to_relay(g, 0).wait_recv)
            when(relays, from_relay(g, 0).start)
        else:
            when(run >= 1, next_run(g, 0).wait_recv)
            when((run >= 1) & has_next, second_run(g).start)
        when(relays, to_relay(g).wait_recv)
        when(relays, from_relay(g).start)

    def key_values(g):
        for mine in (True, False):
            k = 4 * (zlo if mine else 1 - zlo) + g
            keep = kv.at[g, 4 + zlo] if mine else kv_out.at[g]
            part(k).wait_recv()
            part(8 + k).wait_recv()
            in_two(keep, turned(summed(k, False), kg_ref[...]))
            keep[:, 256:384] = summed(8 + k, False).astype(BF16)
        over_pair(g).start()
        when(g < 2, lambda: send_own(g))

    def stage(n):
        when(n < 4, lambda: late_group(n))
        when(n > 0, lambda: key_values(n - 1))

    loop(5, stage)

    query_gain = qg_ref[...] * (QSCALE ** -0.5 * math.log2(math.e))

    def queries(g, mine):
        head = 8 * (zlo if mine else 1 - zlo) + 2 * g
        for i in (0, 1):
            in_two(q_own.at[head + i], turned(summed(head + i, True), query_gain))

    def queries_out(g):
        queries(g, False)
        query_pair(g).start()

    hop(0)
    hop(1)
    loop(4, queries_out)
    forward(0)
    send_own(2)
    hop(2)
    hop(3)
    loop(4, lambda g: queries(g, True))
    loop(16, lambda h: part(h).wait_send())

    row = lax.broadcasted_iota(jnp.int32, (rows, rows), 0)
    col = lax.broadcasted_iota(jnp.int32, (rows, rows), 1)
    causal = col <= row

    def score_steps(slot, g, token_block, q):
        q = q.reshape(2 * rows, 256)
        q_hi, q_lo = q[:, 0:128], q[:, 128:256]
        q = jnp.concatenate([q_hi, q_hi, q_lo, q_lo], axis=1)
        pen = [jnp.where(2 * run - 4 + token_block + m >= 0, 0.0, NEG).astype(F32)
               for m in range(4)]
        best = []

        def score(m):
            keys = kv[g, token_block + m, :, 0:256]
            keys = jnp.concatenate([keys, keys], axis=1)
            out = lax.dot_general(q, keys, (((1,), (1,)), ((), ())), preferred_element_type=F32)
            return out.reshape(2, rows, 256)

        def tile(m):
            if m == 0:
                out = jnp.where(causal[None], score(4), score(0) + pen[0])
            else:
                out = score(m) + pen[m]
            acc[4 * slot + m] = out
            high = jnp.maximum(out[:, :, 0:128], out[:, :, 128:256])
            best.append(jnp.maximum(best[-1], high) if best else high)
            if m == 3:
                top[slot] = jnp.broadcast_to(
                    jnp.max(best[-1], axis=-1, keepdims=True), (2, rows, 128))

        return [functools.partial(tile, m) for m in range(4)]

    def value_steps(slot, g, token_block, keep):
        def one(i):
            high = top[slot, i, :, 0:1]
            w = [jnp.exp2(acc[4 * slot + m, i] - high) for m in range(4)]
            total = jnp.sum((w[0] + w[1]) + (w[2] + w[3]), axis=-1, keepdims=True)
            inv = 1.0 / total
            w = [v * inv for v in w]
            probs = [jnp.where(causal, 0.0, w[0]), w[1], w[2], w[3], jnp.where(causal, w[0], 0.0)]
            probs = jnp.concatenate([p.astype(BF16) for p in probs], axis=1)
            values = kv[g, pl.ds(token_block, 5), :, 256:384].reshape(5 * rows, 128)
            out = jnp.dot(probs, values, preferred_element_type=F32)
            keep[:, 128 * i:128 * i + 128] = out.astype(BF16)

        return [functools.partial(one, i) for i in (0, 1)]

    def columns(g):
        return out_ref.at[:, pl.ds(pl.multiple_of((8 * zlo + 2 * g) * 128, 256), 256)]

    def give(g):
        return remote(result.at[1, g], columns(g), out_send.at[g], out_recv.at[g], pair)

    def keep_own(g):
        return pltpu.make_async_copy(result.at[0, g], columns(g), local_sem.at[5 + g])

    def window(g):
        if g == LAST:
            when(run >= 1, next_run(g, 0).wait_recv)
        when(run >= 1, next_run(g, 1).wait_recv)
        when(run >= 2, from_relay(g, 0).wait_recv if g == LAST else second_run(g).wait_recv)
        when(run >= 2, from_relay(g).wait_recv)

    def score_mine(g):
        return score_steps(0, g, zlo, q_own[pl.ds(8 * zlo + 2 * g, 2)])

    def score_theirs(g):
        return score_steps(1, g, 1 - zlo, q_in[pl.ds(2 * g, 2)])

    def value_mine(g):
        return value_steps(0, g, zlo, result.at[0, g])

    def value_theirs(g):
        return value_steps(1, g, 1 - zlo, result.at[1, g])

    def together(scores, values):
        for n in (0, 4, 1, 2, 5, 3):
            steps = values if n >= 4 else scores
            if steps:
                steps[n % 4]()

    forward(1)
    send_own(3)
    window(0)
    query_pair(0).wait_recv()
    together(score_theirs(0), [])
    for g in range(4):
        together(score_mine(g), value_theirs(g))
        give(g).start()
        if g == 0:
            forward(2)
            forward(3)
        if g < 3:
            window(g + 1)
            query_pair(g + 1).wait_recv()
        together(score_theirs(g + 1) if g < 3 else [], value_mine(g))
        keep_own(g).start()

    for copy in sent:
        copy.wait_send()

    for g in range(4):
        over_pair(g).wait_send()
        query_pair(g).wait_send()
        when(has_next, next_run(g, 0).wait_send)
        when(has_next, next_run(g, 1).wait_send)
        if g == LAST:
            when(has_second, to_relay(g, 0).wait_send)
            when(relays, from_relay(g, 0).wait_send)
        else:
            when((run >= 1) & has_next, second_run(g).wait_send)
        when(has_second, to_relay(g).wait_send)
        when(relays, from_relay(g).wait_send)
        keep_own(g).wait()
        give(g).wait()


def on_device(tokens, norm_gain, w_query, w_keyval, q_gain, k_gain):
    rows, width = tokens.shape[1:]
    quarter, cols = w_query.shape
    heads = cols * lax.axis_size("seq") // q_gain.shape[0]
    half = q_gain.shape[0] // 2
    third = quarter // 3
    place = (lax.axis_index("seq") * rows + jnp.arange(rows)).astype(F32)
    freq = jnp.power(10000.0, -2.0 * (jnp.arange(2 * half) % half).astype(F32) / (2 * half))
    angle = place[:, None] * freq[None, :]
    cos = jnp.cos(angle)
    sin = jnp.where(jnp.arange(2 * half) < half, -1.0, 1.0) * jnp.sin(angle)
    vmem = pl.BlockSpec(memory_space=pltpu.VMEM)
    anyspace = pl.BlockSpec(memory_space=pl.ANY)
    dma = pltpu.SemaphoreType.DMA
    block = pltpu.VMEM((4, 4, 4, third, 128), BF16)
    out = pl.pallas_call(
        layer_kernel,
        name="layer",
        out_shape=jax.ShapeDtypeStruct((rows, heads * 128), BF16),
        in_specs=[anyspace, vmem, vmem, vmem, anyspace, anyspace, vmem, vmem],
        out_specs=vmem,
        scratch_shapes=[
            block, block, block,
            pltpu.VMEM((rows, width), BF16),
            pltpu.VMEM((rows, 128), F32),
            pltpu.VMEM((rows, 128), F32),
            pltpu.VMEM((4, 3, rows, third), BF16),
            pltpu.VMEM((2, 2, 3, rows, third), BF16),
            pltpu.VMEM((heads, 2, rows, 256), F32),
            pltpu.VMEM((2, 2, rows, 128), F32),
            pltpu.VMEM((heads, rows, 256), F32),
            pltpu.VMEM((heads, rows, 256), BF16),
            pltpu.VMEM((heads // 2, rows, 256), BF16),
            pltpu.VMEM((4, rows, 384), BF16),
            pltpu.VMEM((4, 6, rows, 384), BF16),
            pltpu.VMEM((5, rows, 384), BF16),
            pltpu.VMEM((2, 4, rows, 256), BF16),
            dma((12,)), dma((3, 3, 5, 2)), dma((3, 3, 5, 2)),
            dma((2,)), dma((2,)), dma((heads,)), dma((heads,)),
            dma((2, 4)), dma((2, 4)), dma((5, 5)), dma((4, 4)), dma((5,)),
            dma((4,)), dma((4,)),
        ],
        compiler_params=pltpu.CompilerParams(
            collective_id=0, has_side_effects=True, vmem_limit_bytes=62 * 2**20),
    )(tokens[0], norm_gain.reshape(-1, 128), w_query.T, w_keyval.T, cos, sin,
      q_gain[None], k_gain[None])
    return out[None]


def solution(mesh):
    in_specs = (P("fsdp", "seq", None), P(), P("fsdp", "seq"), P("fsdp", "seq"), P(), P())
    out_specs = P("fsdp", "seq", None)
    return jax.shard_map(
        on_device, mesh=mesh, in_specs=in_specs, out_specs=out_specs, check_vma=False
    )
```
